256 devices in a mesh: snap: 16 (over z, y_lo), space: 16 (over x, y_hi, core).
Axes of the slice: x: 4, y: 4 (y_hi: 2, y_lo: 2; y = y_hi * 2 + y_lo), z: 8, core: 2. Of those that a mesh axis runs over, the one named last changes fastest.
Arguments:
- snapshots: bfloat16 [2048, 2, 64, 720], P('snap', None, 'space'), may hold values from -6 to 6
- lon_coeff: float32 [2, 64, 720], P(None, 'space'), may hold values from 0.05 to 0.24
- lat_coeff: float32 [2, 64, 720], P(None, 'space'), may hold values from 0.1 to 0.24
Outputs:
- gram: float32 [2048, 2048], P('snap', 'space')
The draws below stay inside these ranges and needn't reach their ends.
All inputs are finite; a program needn't handle non-finite values.
Results may differ from the reference program's by a relative error of at most 0.00062.
Values may be sent and summed in bfloat16 or wider, within the bound.
A program may use at most 128 MiB of HBM per device.

```python
import math
import jax
import jax.numpy as jnp
from jax import lax

FIELDS = 2
NLON = 720
NLAT = 64
SNAPS = 2048


def steps_of(own_key, dims, cuts, low, largest):
    gain, own = 1.0, jax.random.fold_in(own_key, 6)
    for axis_at, shards_of in cuts:
        draws = jnp.exp(jax.random.uniform(jax.random.fold_in(own, axis_at), (shards_of,), jnp.float32, low / len(cuts), largest / len(cuts)))
        gain = gain * jnp.repeat(draws, dims[axis_at] // shards_of).reshape([-1 if axis == axis_at else 1 for axis in range(len(dims))])
    return gain


def normal_values(stream_key, dims, width, reach, split=(), dtype=jnp.bfloat16):
    loudness = steps_of(stream_key, dims, split, -0.22, 0.18) if split else 1.0
    entries = jax.random.normal(stream_key, dims, jnp.float32) * width * loudness
    return jnp.minimum(jnp.maximum(entries, -reach), reach).astype(dtype)


def setup_inputs(seed: int = 0) -> dict:
    key_of = jax.random.split(jax.random.key(seed), 4)
    snapshots = normal_values(key_of[0], (SNAPS, FIELDS, NLAT, NLON), 1.0, 6.0, ((0, 16), (2, 16)))
    lon_coeff = jnp.clip(jnp.exp(math.log(0.24) - 1.5686159 * jax.random.uniform(key_of[1], (FIELDS, NLAT, NLON), jnp.float32) ** steps_of(key_of[1], (FIELDS, NLAT, NLON), ((1, 16),), -0.2, 0.2)), 0.05, 0.24)
    lat_coeff = jnp.clip(jnp.exp(math.log(0.24) - 0.8754687 * jax.random.uniform(key_of[2], (FIELDS, NLAT, NLON), jnp.float32) ** steps_of(key_of[2], (FIELDS, NLAT, NLON), ((1, 16),), -0.2, 0.2)), 0.1, 0.24)
    return {"snapshots": snapshots, "lon_coeff": lon_coeff, "lat_coeff": lat_coeff}


def reference(snapshots, lon_coeff, lat_coeff):
    values = snapshots.astype(jnp.float32)
    lon_part = jnp.roll(values, 1, axis=3) + jnp.roll(values, -1, axis=3) - 2.0 * values
    padded = jnp.pad(values, ((0, 0), (0, 0), (1, 1), (0, 0)))
    lat_part = padded[:, :, 2:] + padded[:, :, :-2] - 2.0 * values
    smooth = values + lon_coeff * lon_part + lat_coeff * lat_part
    rows = jnp.arange(NLAT).astype(jnp.float32)
    angle = (45.0 + 0.5 * (rows + 0.5 - NLAT / 2.0)) * (math.pi / 180.0)
    cosine = jnp.cos(angle)
    total = FIELDS * NLON * jnp.sum(cosine)
    factor = jnp.sqrt(cosine) * total ** (-0.25)
    scaled = (smooth * factor[:, None]).astype(jnp.bfloat16).reshape(smooth.shape[0], -1)
    return lax.dot_general(scaled, scaled, (((1,), (1,)), ((), ())), preferred_element_type=jnp.float32)
```

```python
import functools
import math

import jax
import jax.numpy as jnp
import numpy as np
from jax import lax
from jax.experimental import pallas as pl
from jax.experimental.pallas import tpu as pltpu
from jax.sharding import PartitionSpec as P

MESH = pl.DeviceIdType.MESH
NLON = 720
KPAD = 1536
B = 128
CH = 144


def row_factors(fields, nlat, nlon):
    lat = (45.0 + 0.5 * (np.arange(nlat) + 0.5 - nlat / 2.0)) * (math.pi / 180.0)
    cosine = np.cos(lat)
    total = fields * nlon * cosine.sum()
    return (np.sqrt(cosine) * total ** (-0.25)).astype(np.float32)


def kernel(x_ref, coef_ref, fac_ref, o_ref,
           halo, v32, sc, rows, a2, part, xin, q, yin, fin, zin, mout, minb,
           halo_s, halo_r, loc_s, z_s, z_r, y_s, y_r, c_s, c_r, x_s, x_r, h_s, h_r, f_s, f_r, m_s, m_r):
    snap = lax.axis_index("snap")
    space = lax.axis_index("space")
    z, yl = snap // 2, snap % 2
    xx, yh, core = space // 4, (space // 2) % 2, space % 2
    m_me = space // 2
    same = (core == yl).astype(jnp.int32)
    nb = 4 + same
    kk0 = 1 - same
    off = jnp.where(same == 1, 0, yl)

    def copy(src, dst, ss, rs, dev):
        return pltpu.make_async_remote_copy(
            src_ref=src, dst_ref=dst, send_sem=ss, recv_sem=rs, device_id=dev, device_id_type=MESH)

    up_dev = (snap, jnp.maximum(space - 1, 0))
    dn_dev = (snap, jnp.minimum(space + 1, 15))
    y_dev = (z * 2 + 1 - yl, space)
    c_dev = (snap, m_me * 2 + 1 - core)
    h_dev = (snap, xx * 4 + (1 - yh) * 2 + core)
    m_dev = (space, snap)

    barrier = pltpu.get_barrier_semaphore()

    def greet(dev):
        pl.semaphore_signal(barrier, inc=1, device_id=dev, device_id_type=MESH)

    for dz in range(1, 8):
        greet((((z + dz) % 8) * 2 + yl, space))
    for dx in range(1, 4):
        greet((snap, ((xx + dx) % 4) * 4 + yh * 2 + core))
    greet(y_dev)
    greet(c_dev)
    greet(h_dev)

    @pl.when(space > 0)
    def _():
        greet(up_dev)

    @pl.when(space < 15)
    def _():
        greet(dn_dev)

    @pl.when(snap != space)
    def _():
        greet(m_dev)

    pl.semaphore_wait(
        barrier,
        13 + (space > 0).astype(jnp.int32) + (space < 15).astype(jnp.int32) + (snap != space).astype(jnp.int32))

    def halo_down(f):
        return copy(x_ref.at[4 * f + 3], halo.at[0, f], halo_s.at[0, f], halo_r.at[0, f], dn_dev)

    def halo_up(f):
        return copy(x_ref.at[4 * f], halo.at[1, f], halo_s.at[1, f], halo_r.at[1, f], up_dev)

    @pl.when(space < 15)
    def _():
        for f in range(2):
            halo_down(f).start()

    @pl.when(space > 0)
    def _():
        for f in range(2):
            halo_up(f).start()

    @pl.when(space == 0)
    def _():
        halo[0] = jnp.zeros((2, NLON, B), jnp.bfloat16)

    @pl.when(space == 15)
    def _():
        halo[1] = jnp.zeros((2, NLON, B), jnp.bfloat16)

    def slot(yy, zz, cc):
        return rows.at[yy, zz, pl.ds(pl.multiple_of(cc * NLON, 16), NLON), :]

    def stencil(j):
        f, row = divmod(j, 4)
        v = x_ref[j].astype(jnp.float32)
        v32[j, pl.ds(8, NLON), :] = v
        v32[j, 7:8, :] = v[NLON - 1:, :]
        v32[j, NLON + 8:NLON + 9, :] = v[:1, :]
        scale = fac_ref[space * 4 + row]
        for s in range(0, NLON, CH):
            a = v32[j, pl.ds(8 + s, CH), :]
            west = v32[j, pl.ds(7 + s, CH), :]
            east = v32[j, pl.ds(9 + s, CH), :]
            if row == 0:
                north = halo[0, f, pl.ds(s, CH), :]
            else:
                north = x_ref[j - 1, pl.ds(s, CH), :]
            if row == 3:
                south = halo[1, f, pl.ds(s, CH), :]
            else:
                south = x_ref[j + 1, pl.ds(s, CH), :]
            lon_part = west + east - 2.0 * a
            lat_part = south.astype(jnp.float32) + north.astype(jnp.float32) - 2.0 * a
            smooth = a + coef_ref[pl.ds(s, CH), j:j + 1] * lon_part + coef_ref[pl.ds(s, CH), 8 + j:9 + j] * lat_part
            sc[j, pl.ds(s, CH), :] = (smooth * scale).astype(jnp.bfloat16)

    def z_copy(j):
        return copy(sc.at[j], slot(yl, z, core), z_s.at[j], z_r.at[z], (j * 2 + yl, space))

    def local_copy(j):
        return pltpu.make_async_copy(sc.at[j], slot(yl, z, core), loc_s)

    def z_start(j):
        @pl.when(z == j)
        def _():
            local_copy(j).start()

        @pl.when(z != j)
        def _():
            z_copy(j).start()

    rows[:, :, 2 * NLON:, :] = jnp.zeros((2, 8, KPAD - 2 * NLON, B), jnp.bfloat16)

    last = None
    for j in (1, 2, 5, 6):
        stencil(j)
        if last is not None:
            z_start(last)
        last = j

    @pl.when(space > 0)
    def _():
        for f in range(2):
            halo_down(f).wait_recv()

    @pl.when(space < 15)
    def _():
        for f in range(2):
            halo_up(f).wait_recv()

    for j in (0, 3, 4, 7):
        stencil(j)
        z_start(last)
        last = j
    z_start(last)

    def near(i):
        return (z + 8 + ((i + 1) // 2) * (2 * (i % 2) - 1)) % 8

    def y_copy(zz):
        return copy(slot(yl, zz, core), slot(yl, zz, core), y_s.at[zz], y_r.at[zz], y_dev)

    def y_arrive(zz):
        copy(slot(1 - yl, zz, core), slot(1 - yl, zz, core), y_s.at[zz], y_r.at[zz], y_dev).wait_recv()

    def c_copy(yy, zz):
        return copy(slot(yy, zz, core), slot(yy, zz, core), c_s.at[yy, zz], c_r.at[yy, zz], c_dev)

    def c_arrive(yy, zz):
        copy(slot(yy, zz, 1 - core), slot(yy, zz, 1 - core), c_s.at[yy, zz], c_r.at[yy, zz], c_dev).wait_recv()

    def turn(zz):
        c_arrive(yl, zz)
        t = rows[yl, zz].T
        a2[pl.ds(pl.multiple_of(zz * B, B), B), :] = t
        a2[pl.ds(pl.multiple_of(zz * B + 8 * B, B), B), :] = t

    def step(i, carry):
        zz = near(i)

        @pl.when(i == 0)
        def _():
            local_copy(0).wait()

        @pl.when(i > 0)
        def _():
            copy(sc.at[0], slot(yl, zz, core), z_s.at[0], z_r.at[zz], (snap, space)).wait_recv()

        y_copy(zz).start()
        c_copy(yl, zz).start()

        @pl.when(i > 0)
        def _():
            before = near(i - 1)
            y_arrive(before)
            c_copy(1 - yl, before).start()
            turn(before)

        return carry

    lax.fori_loop(0, 8, step, 0)
    y_arrive(near(7))
    c_copy(1 - yl, near(7)).start()
    turn(near(7))

    def arrive(zz, carry):
        c_arrive(1 - yl, zz)
        return carry

    lax.fori_loop(0, 8, arrive, 0)

    def blk(kk):
        return pl.ds(pl.multiple_of(kk * B, B), B)

    def x_copy(m, kk):
        return copy(part.at[m, blk(kk), :], xin.at[xx, m % 2, blk(kk), :], x_s.at[m, kk],
                    x_r.at[xx, m % 2, kk], (snap, (m // 2) * 4 + yh * 2 + core))

    def m_of(t):
        return ((xx + t // 2 + 1) % 4) * 2 + t % 2

    def product(t, carry):
        m = m_of(t)
        start = pl.multiple_of(((m + 8 - 4 - off) % 8) * B, B)
        part[m] = jnp.dot(a2[pl.ds(start, 5 * B), :], rows[core, m], preferred_element_type=jnp.float32)

        @pl.when((t > 0) & (t < 7))
        def _():
            def send(kk, c):
                x_copy(m_of(t - 1), kk).start()
                return c

            lax.fori_loop(kk0, 5, send, 0)

        return carry

    lax.fori_loop(0, 8, product, 0)

    def x_sum(yy, kk):
        m = 2 * xx + yy
        total = part[m, blk(kk), :]
        for dx in range(1, 4):
            src = (xx + dx) % 4
            copy(part.at[0, blk(kk), :], xin.at[src, yy, blk(kk), :], x_s.at[m, kk], x_r.at[src, yy, kk],
                 (snap, space)).wait_recv()
            total = total + xin[src, yy, blk(kk), :]
        return total

    def h_copy(kk):
        return copy(q.at[blk(kk), :], yin.at[blk(kk), :], h_s.at[kk], h_r.at[kk], h_dev)

    def other_half(kk, carry):
        q[blk(kk), :] = x_sum(1 - yh, kk)

        @pl.when(kk > kk0)
        def _():
            h_copy(kk - 1).start()

        return carry

    lax.fori_loop(kk0, 5, other_half, 0)

    def own_half(kk, carry):
        fin[blk(kk), :] = x_sum(yh, kk)

        @pl.when(kk == kk0)
        def _():
            h_copy(4).start()

        return carry

    lax.fori_loop(kk0, 5, own_half, 0)

    def z_of(kk):
        return (m_me + 8 - 4 + kk - off) % 8

    def f_copy(kk):
        return copy(fin.at[blk(kk), :], zin.at[z], f_s.at[kk], f_r.at[z], (z_of(kk) * 2 + yl, space))

    def f_start(kk):
        @pl.when(z_of(kk) != z)
        def _():
            f_copy(kk).start()

    def add_half(kk, carry):
        h_copy(kk).wait_recv()
        fin[blk(kk), :] = fin[blk(kk), :] + yin[blk(kk), :]

        @pl.when(kk > kk0)
        def _():
            f_start(kk - 1)

        return carry

    lax.fori_loop(kk0, 5, add_half, 0)
    f_start(4)

    k_me = (m_me + 8 - off - z) % 8
    d_me = 2 * (k_me + off) + core - yl
    mine = k_me < nb
    sends_mirror = mine & (d_me >= 1) & (d_me <= 7)
    mirror = copy(mout, minb, m_s, m_r, m_dev)

    @pl.when(mine)
    def _():
        total = fin[blk(4 - k_me), :]
        for dz in range(1, 8):
            zz = (z + dz) % 8
            copy(fin.at[blk(0), :], zin.at[zz], f_s.at[0], f_r.at[zz], (snap, space)).wait_recv()
            total = total + zin[zz]
        mout[...] = total
        o_ref[...] = total

    @pl.when(sends_mirror)
    def _():
        mirror.start()

    @pl.when(jnp.logical_not(mine))
    def _():
        mirror.wait_recv()
        o_ref[...] = minb[...].T

    @pl.when(space < 15)
    def _():
        for f in range(2):
            halo_down(f).wait_send()

    @pl.when(space > 0)
    def _():
        for f in range(2):
            halo_up(f).wait_send()

    for j in range(8):
        @pl.when(z != j)
        def _():
            z_copy(j).wait_send()

    def drain(zz, carry):
        y_copy(zz).wait_send()
        c_copy(0, zz).wait_send()
        c_copy(1, zz).wait_send()
        return carry

    lax.fori_loop(0, 8, drain, 0)

    def drain_blocks(kk, carry):
        for t in range(6):
            x_copy(m_of(t), kk).wait_send()
        h_copy(kk).wait_send()

        @pl.when(z_of(kk) != z)
        def _():
            f_copy(kk).wait_send()

        return carry

    lax.fori_loop(kk0, 5, drain_blocks, 0)

    @pl.when(sends_mirror)
    def _():
        mirror.wait_send()


def shards(factors, snapshots, lon_coeff, lat_coeff):
    x = jnp.transpose(snapshots, (1, 2, 3, 0)).reshape(8, NLON, B)
    coef = jnp.concatenate([lon_coeff.reshape(8, NLON), lat_coeff.reshape(8, NLON)], axis=0).T
    dma = pltpu.SemaphoreType.DMA
    vmem = pl.BlockSpec(memory_space=pltpu.VMEM)
    bf, f32 = jnp.bfloat16, jnp.float32
    return pl.pallas_call(
        kernel,
        out_shape=jax.ShapeDtypeStruct((B, B), f32),
        in_specs=[vmem, vmem, pl.BlockSpec(memory_space=pltpu.SMEM)],
        out_specs=vmem,
        scratch_shapes=[
            pltpu.VMEM((2, 2, NLON, B), bf),
            pltpu.VMEM((8, NLON + 16, B), f32),
            pltpu.VMEM((8, NLON, B), bf),
            pltpu.VMEM((2, 8, KPAD, B), bf),
            pltpu.VMEM((16 * B, KPAD), bf),
            pltpu.VMEM((8, 5 * B, B), f32),
            pltpu.VMEM((4, 2, 5 * B, B), f32),
            pltpu.VMEM((5 * B, B), f32),
            pltpu.VMEM((5 * B, B), f32),
            pltpu.VMEM((5 * B, B), f32),
            pltpu.VMEM((8, B, B), f32),
            pltpu.VMEM((B, B), f32),
            pltpu.VMEM((B, B), f32),
            dma((2, 2)), dma((2, 2)), dma,
            dma((8,)), dma((8,)),
            dma((8,)), dma((8,)),
            dma((2, 8)), dma((2, 8)),
            dma((8, 5)), dma((4, 2, 5)),
            dma((5,)), dma((5,)),
            dma((5,)), dma((8,)),
            dma, dma,
        ],
        compiler_params=pltpu.CompilerParams(collective_id=0, has_side_effects=True),
        name="gram",
    )(x, coef, jnp.asarray(factors))


def solution(mesh):
    factors = row_factors(2, 64, NLON)
    return jax.shard_map(
        functools.partial(shards, factors),
        mesh=mesh,
        in_specs=(P("snap", None, "space", None), P(None, "space", None), P(None, "space", None)),
        out_specs=P("snap", "space"),
        check_vma=False,
    )
```

```python
import functools
import math

import jax
import jax.numpy as jnp
import numpy as np
from jax import lax
from jax.experimental import pallas as pl
from jax.experimental.pallas import tpu as pltpu
from jax.sharding import PartitionSpec as P

MESH = pl.DeviceIdType.MESH
NLON = 720
KPAD = 1536
B = 128
CH = 144


def row_factors(fields, nlat, nlon):
    lat = (45.0 + 0.5 * (np.arange(nlat) + 0.5 - nlat / 2.0)) * (math.pi / 180.0)
    cosine = np.cos(lat)
    total = fields * nlon * cosine.sum()
    return (np.sqrt(cosine) * total ** (-0.25)).astype(np.float32)


def kernel(x_ref, lon_ref, lat_ref, fac_ref, o_ref,
           coef, halo, v32, sc, rows, a2, part, xin, q, yin, fin, zin, mout, minb,
           halo_s, halo_r, loc_s, z_s, z_r, y_s, y_r, c_s, c_r, x_s, x_r, h_s, h_r, f_s, f_r, m_s, m_r):
    snap = lax.axis_index("snap")
    space = lax.axis_index("space")
    z, yl = snap // 2, snap % 2
    xx, yh, core = space // 4, (space // 2) % 2, space % 2
    m_me = space // 2
    same = (core == yl).astype(jnp.int32)
    nb = 4 + same
    kk0 = 1 - same
    off = jnp.where(same == 1, 0, yl)

    def copy(src, dst, ss, rs, dev):
        return pltpu.make_async_remote_copy(
            src_ref=src, dst_ref=dst, send_sem=ss, recv_sem=rs, device_id=dev, device_id_type=MESH)

    up_dev = (snap, jnp.maximum(space - 1, 0))
    dn_dev = (snap, jnp.minimum(space + 1, 15))
    y_dev = (z * 2 + 1 - yl, space)
    c_dev = (snap, m_me * 2 + 1 - core)
    h_dev = (snap, xx * 4 + (1 - yh) * 2 + core)
    m_dev = (space, snap)

    barrier = pltpu.get_barrier_semaphore()

    def greet(dev):
        pl.semaphore_signal(barrier, inc=1, device_id=dev, device_id_type=MESH)

    for dz in range(1, 8):
        greet((((z + dz) % 8) * 2 + yl, space))
    for dx in range(1, 4):
        greet((snap, ((xx + dx) % 4) * 4 + yh * 2 + core))
    greet(y_dev)
    greet(c_dev)
    greet(h_dev)

    @pl.when(space > 0)
    def _():
        greet(up_dev)

    @pl.when(space < 15)
    def _():
        greet(dn_dev)

    @pl.when(snap != space)
    def _():
        greet(m_dev)

    def halo_down(f):
        return copy(x_ref.at[4 * f + 3], halo.at[0, f], halo_s.at[0, f], halo_r.at[0, f], dn_dev)

    def halo_up(f):
        return copy(x_ref.at[4 * f], halo.at[1, f], halo_s.at[1, f], halo_r.at[1, f], up_dev)

    def slot(yy, zz, cc):
        return rows.at[yy, zz, pl.ds(pl.multiple_of(cc * NLON, 16), NLON), :]

    def stencil(j):
        f, row = divmod(j, 4)
        v = x_ref[j].astype(jnp.float32)
        v32[j, pl.ds(8, NLON), :] = v
        v32[j, 7:8, :] = v[NLON - 1:, :]
        v32[j, NLON + 8:NLON + 9, :] = v[:1, :]
        scale = fac_ref[space * 4 + row]
        for s in range(0, NLON, CH):
            a = v32[j, pl.ds(8 + s, CH), :]
            west = v32[j, pl.ds(7 + s, CH), :]
            east = v32[j, pl.ds(9 + s, CH), :]
            if row == 0:
                north = halo[0, f, pl.ds(s, CH), :]
            else:
                north = x_ref[j - 1, pl.ds(s, CH), :]
            if row == 3:
                south = halo[1, f, pl.ds(s, CH), :]
            else:
                south = x_ref[j + 1, pl.ds(s, CH), :]
            lon_part = west + east - 2.0 * a
            lat_part = south.astype(jnp.float32) + north.astype(jnp.float32) - 2.0 * a
            smooth = a + coef[pl.ds(s, CH), j:j + 1] * lon_part + coef[pl.ds(s, CH), 8 + j:9 + j] * lat_part
            sc[j, pl.ds(s, CH), :] = (smooth * scale).astype(jnp.bfloat16)

    def j_of(zz):
        return (zz + 8 - core) % 8

    def z_copy(zz):
        return copy(sc.at[j_of(zz)], slot(yl, z, core), z_s.at[zz], z_r.at[z], (zz * 2 + yl, space))

    def local_copy():
        return pltpu.make_async_copy(sc.at[j_of(z)], slot(yl, z, core), loc_s)

    def near(i):
        return (z + 8 + ((i + 1) // 2) * (2 * (i % 2) - 1)) % 8

    coef[...] = jnp.concatenate([lon_ref[0], lon_ref[1], lat_ref[0], lat_ref[1]], axis=0).T
    rows[:, :, 2 * NLON:, :] = jnp.zeros((2, 8, KPAD - 2 * NLON, B), jnp.bfloat16)

    @pl.when(space == 0)
    def _():
        halo[0] = jnp.zeros((2, NLON, B), jnp.bfloat16)

    @pl.when(space == 15)
    def _():
        halo[1] = jnp.zeros((2, NLON, B), jnp.bfloat16)

    for j in (1, 2, 5, 6):
        stencil(j)

    pl.semaphore_wait(
        barrier,
        13 + (space > 0).astype(jnp.int32) + (space < 15).astype(jnp.int32) + (snap != space).astype(jnp.int32))

    @pl.when(core == 0)
    def _():
        for f in range(2):
            halo_down(f).start()

        @pl.when(space > 0)
        def _():
            for f in range(2):
                halo_up(f).start()

        for f in range(2):
            halo_up(f).wait_recv()
        stencil(3)
        stencil(7)

    @pl.when(core == 1)
    def _():
        for f in range(2):
            halo_up(f).start()

        @pl.when(space < 15)
        def _():
            for f in range(2):
                halo_down(f).start()

        for f in range(2):
            halo_down(f).wait_recv()
        stencil(0)
        stencil(4)

    def z_start(i, carry):
        zz = near(i)

        @pl.when(zz % 4 != 0)
        def _():
            @pl.when(i == 0)
            def _():
                local_copy().start()

            @pl.when(i > 0)
            def _():
                z_copy(zz).start()

        return carry

    lax.fori_loop(0, 8, z_start, 0)

    def y_copy(zz):
        return copy(slot(yl, zz, core), slot(yl, zz, core), y_s.at[zz], y_r.at[zz], y_dev)

    def y_arrive(zz):
        copy(slot(1 - yl, zz, core), slot(1 - yl, zz, core), y_s.at[zz], y_r.at[zz], y_dev).wait_recv()

    def c_copy(yy, zz):
        return copy(slot(yy, zz, core), slot(yy, zz, core), c_s.at[yy, zz], c_r.at[yy, zz], c_dev)

    def c_arrive(yy, zz):
        copy(slot(yy, zz, 1 - core), slot(yy, zz, 1 - core), c_s.at[yy, zz], c_r.at[yy, zz], c_dev).wait_recv()

    def turn(zz):
        c_arrive(yl, zz)
        t = rows[yl, zz].T
        a2[pl.ds(pl.multiple_of(zz * B, B), B), :] = t
        a2[pl.ds(pl.multiple_of(zz * B + 8 * B, B), B), :] = t

    def step(i, carry):
        zz = near(i)

        @pl.when(i == 0)
        def _():
            local_copy().wait()

        @pl.when(i > 0)
        def _():
            copy(sc.at[0], slot(yl, zz, core), z_s.at[0], z_r.at[zz], (snap, space)).wait_recv()

        y_copy(zz).start()
        c_copy(yl, zz).start()

        @pl.when(i > 0)
        def _():
            before = near(i - 1)
            y_arrive(before)
            c_copy(1 - yl, before).start()
            turn(before)

        return carry

    early = jnp.where(z % 4 == 0, 0, 3)
    lax.fori_loop(0, early, step, 0)

    @pl.when(core == 0)
    def _():
        @pl.when(space > 0)
        def _():
            for f in range(2):
                halo_down(f).wait_recv()

        stencil(0)
        stencil(4)

    @pl.when(core == 1)
    def _():
        @pl.when(space < 15)
        def _():
            for f in range(2):
                halo_up(f).wait_recv()

        stencil(3)
        stencil(7)

    def z_start_late(i, carry):
        zz = near(i)

        @pl.when(zz % 4 == 0)
        def _():
            @pl.when(i == 0)
            def _():
                local_copy().start()

            @pl.when(i > 0)
            def _():
                z_copy(zz).start()

        return carry

    lax.fori_loop(0, 8, z_start_late, 0)
    lax.fori_loop(early, 8, step, 0)
    y_arrive(near(7))
    c_copy(1 - yl, near(7)).start()
    turn(near(7))

    def arrive(zz, carry):
        c_arrive(1 - yl, zz)
        return carry

    lax.fori_loop(0, 8, arrive, 0)

    def blk(kk):
        return pl.ds(pl.multiple_of(kk * B, B), B)

    def x_copy(m, kk):
        return copy(part.at[m, blk(kk), :], xin.at[xx, m % 2, blk(kk), :], x_s.at[m, kk],
                    x_r.at[xx, m % 2, kk], (snap, (m // 2) * 4 + yh * 2 + core))

    def m_of(t):
        return ((xx + t // 2 + 1) % 4) * 2 + t % 2

    def product(t, carry):
        m = m_of(t)
        start = pl.multiple_of(((m + 8 - 4 - off) % 8) * B, B)
        part[m] = jnp.dot(a2[pl.ds(start, 5 * B), :], rows[core, m], preferred_element_type=jnp.float32)

        @pl.when((t > 0) & (t < 7))
        def _():
            def send(kk, c):
                x_copy(m_of(t - 1), kk).start()
                return c

            lax.fori_loop(kk0, 5, send, 0)

        return carry

    lax.fori_loop(0, 8, product, 0)

    def x_sum(yy, kk):
        m = 2 * xx + yy
        total = part[m, blk(kk), :]
        for dx in range(1, 4):
            src = (xx + dx) % 4
            copy(part.at[0, blk(kk), :], xin.at[src, yy, blk(kk), :], x_s.at[m, kk], x_r.at[src, yy, kk],
                 (snap, space)).wait_recv()
            total = total + xin[src, yy, blk(kk), :]
        return total

    def h_copy(kk):
        return copy(q.at[blk(kk), :], yin.at[blk(kk), :], h_s.at[kk], h_r.at[kk], h_dev)

    def other_half(kk, carry):
        q[blk(kk), :] = x_sum(1 - yh, kk)

        @pl.when(kk > kk0)
        def _():
            h_copy(kk - 1).start()

        return carry

    lax.fori_loop(kk0, 5, other_half, 0)

    def own_half(kk, carry):
        fin[blk(kk), :] = x_sum(yh, kk)

        @pl.when(kk == kk0)
        def _():
            h_copy(4).start()

        return carry

    lax.fori_loop(kk0, 5, own_half, 0)

    def z_of(kk):
        return (m_me + 8 - 4 + kk - off) % 8

    def f_copy(kk):
        return copy(fin.at[blk(kk), :], zin.at[z], f_s.at[kk], f_r.at[z], (z_of(kk) * 2 + yl, space))

    def f_start(kk):
        @pl.when(z_of(kk) != z)
        def _():
            f_copy(kk).start()

    def add_half(kk, carry):
        h_copy(kk).wait_recv()
        fin[blk(kk), :] = fin[blk(kk), :] + yin[blk(kk), :]

        @pl.when(kk > kk0)
        def _():
            f_start(kk - 1)

        return carry

    lax.fori_loop(kk0, 5, add_half, 0)
    f_start(4)

    k_me = (m_me + 8 - off - z) % 8
    d_me = 2 * (k_me + off) + core - yl
    mine = k_me < nb
    sends_mirror = mine & (d_me >= 1) & (d_me <= 7)
    mirror = copy(mout, minb, m_s, m_r, m_dev)

    @pl.when(mine)
    def _():
        total = fin[blk(4 - k_me), :]
        for dz in range(1, 8):
            zz = (z + dz) % 8
            copy(fin.at[blk(0), :], zin.at[zz], f_s.at[0], f_r.at[zz], (snap, space)).wait_recv()
            total = total + zin[zz]
        mout[...] = total
        o_ref[...] = total

    @pl.when(sends_mirror)
    def _():
        mirror.start()

    @pl.when(jnp.logical_not(mine))
    def _():
        mirror.wait_recv()
        o_ref[...] = minb[...].T

    @pl.when(space < 15)
    def _():
        for f in range(2):
            halo_down(f).wait_send()

    @pl.when(space > 0)
    def _():
        for f in range(2):
            halo_up(f).wait_send()

    for dz in range(1, 8):
        z_copy((z + dz) % 8).wait_send()

    def drain(zz, carry):
        y_copy(zz).wait_send()
        c_copy(0, zz).wait_send()
        c_copy(1, zz).wait_send()
        return carry

    lax.fori_loop(0, 8, drain, 0)

    def drain_blocks(kk, carry):
        for t in range(6):
            x_copy(m_of(t), kk).wait_send()
        h_copy(kk).wait_send()

        @pl.when(z_of(kk) != z)
        def _():
            f_copy(kk).wait_send()

        return carry

    lax.fori_loop(kk0, 5, drain_blocks, 0)

    @pl.when(sends_mirror)
    def _():
        mirror.wait_send()


def shards(factors, snapshots, lon_coeff, lat_coeff):
    x = jnp.transpose(snapshots, (1, 2, 3, 0)).reshape(8, NLON, B)
    dma = pltpu.SemaphoreType.DMA
    vmem = pl.BlockSpec(memory_space=pltpu.VMEM)
    bf, f32 = jnp.bfloat16, jnp.float32
    return pl.pallas_call(
        kernel,
        out_shape=jax.ShapeDtypeStruct((B, B), f32),
        in_specs=[vmem, vmem, vmem, pl.BlockSpec(memory_space=pltpu.SMEM)],
        out_specs=vmem,
        scratch_shapes=[
            pltpu.VMEM((NLON, 16), f32),
            pltpu.VMEM((2, 2, NLON, B), bf),
            pltpu.VMEM((8, NLON + 16, B), f32),
            pltpu.VMEM((8, NLON, B), bf),
            pltpu.VMEM((2, 8, KPAD, B), bf),
            pltpu.VMEM((16 * B, KPAD), bf),
            pltpu.VMEM((8, 5 * B, B), f32),
            pltpu.VMEM((4, 2, 5 * B, B), f32),
            pltpu.VMEM((5 * B, B), f32),
            pltpu.VMEM((5 * B, B), f32),
            pltpu.VMEM((5 * B, B), f32),
            pltpu.VMEM((8, B, B), f32),
            pltpu.VMEM((B, B), f32),
            pltpu.VMEM((B, B), f32),
            dma((2, 2)), dma((2, 2)), dma,
            dma((8,)), dma((8,)),
            dma((8,)), dma((8,)),
            dma((2, 8)), dma((2, 8)),
            dma((8, 5)), dma((4, 2, 5)),
            dma((5,)), dma((5,)),
            dma((5,)), dma((8,)),
            dma, dma,
        ],
        compiler_params=pltpu.CompilerParams(collective_id=0, has_side_effects=True),
        name="gram",
    )(x, lon_coeff, lat_coeff, jnp.asarray(factors))


def solution(mesh):
    factors = row_factors(2, 64, NLON)
    return jax.shard_map(
        functools.partial(shards, factors),
        mesh=mesh,
        in_specs=(P("snap", None, "space", None), P(None, "space", None), P(None, "space", None)),
        out_specs=P("snap", "space"),
        check_vma=False,
    )
```

```python
import functools
import math

import jax
import jax.numpy as jnp
import numpy as np
from jax import lax
from jax.experimental import pallas as pl
from jax.experimental.pallas import tpu as pltpu
from jax.sharding import PartitionSpec as P

MESH = pl.DeviceIdType.MESH
NLON = 720
KPAD = 1536
B = 128
CH = 144
QT = B // 4
EARLY, LATE = 528, 192
ORDER = [(word[:1], int(word[1:])) for word in (
    "l0", "z1", "z2", "t0", "y0", "w1", "w2", "z3", "z4", "t1", "y1", "t2", "s0", "y2", "w3", "w4", "z5", "z6",
    "h0", "L0", "Z1", "Z2", "Z3", "Z4", "Z5", "Z6", "Z7", "T0", "Y0", "t3", "s1", "y3", "t4", "s2", "y4", "S0",
    "T1", "Y1", "T2", "Y2", "p0", "s3", "S1", "p1", "S2", "p2", "T3", "Y3", "T4", "Y4", "w5", "w6", "z7", "t5",
    "y5", "t6", "y6", "s4", "S3", "p3", "x0", "S4", "p4", "x1", "T5", "Y5", "T6", "Y6", "T7", "t7", "y7", "Y7",
    "s5", "S5", "p5", "x2", "x3", "s6", "S6", "p6", "x4", "x5", "s7", "S7", "p7", "x6", "x7",
)]


def row_factors(fields, nlat, nlon):
    lat = (45.0 + 0.5 * (np.arange(nlat) + 0.5 - nlat / 2.0)) * (math.pi / 180.0)
    cosine = np.cos(lat)
    total = fields * nlon * cosine.sum()
    return (np.sqrt(cosine) * total ** (-0.25)).astype(np.float32)


def kernel(x_ref, lon_ref, lat_ref, fac_ref, o_ref,
           coef, halo, v32, sc, rows, a2, part, xin, fin, zin, tot, obuf, minb,
           halo_s, halo_r, loc_s, z_s, z_r, y_s, y_r, c_s, c_r, x_s, x_r, f_s, f_r,
           o_s, o_r, m_s, m_r):
    snap = lax.axis_index("snap")
    space = lax.axis_index("space")
    z, yl = snap // 2, snap % 2
    xx, yh, core = space // 4, (space // 2) % 2, space % 2
    m_me = space // 2
    same = (core == yl).astype(jnp.int32)
    nb = 4 + same
    kk0 = 1 - same
    off = jnp.where(same == 1, 0, yl)

    def copy(src, dst, ss, rs, dev):
        return pltpu.make_async_remote_copy(
            src_ref=src, dst_ref=dst, send_sem=ss, recv_sem=rs, device_id=dev, device_id_type=MESH)

    up_dev = (snap, jnp.maximum(space - 1, 0))
    dn_dev = (snap, jnp.minimum(space + 1, 15))
    y_dev = (z * 2 + 1 - yl, space)
    c_dev = (snap, m_me * 2 + 1 - core)
    h_dev = (snap, xx * 4 + (1 - yh) * 2 + core)

    barrier = pltpu.get_barrier_semaphore()

    def greet(dev):
        pl.semaphore_signal(barrier, inc=1, device_id=dev, device_id_type=MESH)

    for dz in range(1, 8):
        greet((((z + dz) % 8) * 2 + yl, space))
        greet((((z + dz) % 8) * 2 + yl, h_dev[1]))
    for dx in range(1, 4):
        greet((snap, ((xx + dx) % 4) * 4 + yh * 2 + core))
    greet(y_dev)
    greet(c_dev)
    greet(h_dev)

    @pl.when(space > 0)
    def _():
        greet(up_dev)

    @pl.when(space < 15)
    def _():
        greet(dn_dev)

    def halo_down(f):
        return copy(x_ref.at[4 * f + 3], halo.at[0, f], halo_s.at[0, f], halo_r.at[0, f], dn_dev)

    def halo_up(f):
        return copy(x_ref.at[4 * f], halo.at[1, f], halo_s.at[1, f], halo_r.at[1, f], up_dev)

    def span(late):
        return LATE if late else EARLY

    def slot(yy, zz, cc, late):
        return rows.at[yy, zz, pl.ds(pl.multiple_of(cc * NLON + late * EARLY, 16), span(late)), :]

    def stencil(j, place):
        f, row = divmod(j, 4)
        v = x_ref[j].astype(jnp.float32)
        v32[j, pl.ds(8, NLON), :] = v
        v32[j, 7:8, :] = v[NLON - 1:, :]
        v32[j, NLON + 8:NLON + 9, :] = v[:1, :]
        scale = fac_ref[space * 4 + row]
        for s in range(0, NLON, CH):
            a = v32[j, pl.ds(8 + s, CH), :]
            west = v32[j, pl.ds(7 + s, CH), :]
            east = v32[j, pl.ds(9 + s, CH), :]
            if row == 0:
                north = halo[0, f, pl.ds(s, CH), :]
            else:
                north = x_ref[j - 1, pl.ds(s, CH), :]
            if row == 3:
                south = halo[1, f, pl.ds(s, CH), :]
            else:
                south = x_ref[j + 1, pl.ds(s, CH), :]
            lon_part = west + east - 2.0 * a
            lat_part = south.astype(jnp.float32) + north.astype(jnp.float32) - 2.0 * a
            smooth = a + coef[pl.ds(s, CH), j:j + 1] * lon_part + coef[pl.ds(s, CH), 8 + j:9 + j] * lat_part
            sc[pl.ds(place * NLON + s, CH), :] = (smooth * scale).astype(jnp.bfloat16)

    def mine_for(zz, late):
        return sc.at[pl.ds(pl.multiple_of(late * 8 * EARLY + zz * span(late), 16), span(late)), :]

    def z_copy(zz, late):
        return copy(mine_for(zz, late), slot(yl, z, core, late), z_s.at[late, zz], z_r.at[late, z],
                    (zz * 2 + yl, space))

    def local_copy(late):
        return pltpu.make_async_copy(mine_for(z, late), slot(yl, z, core, late), loc_s.at[late])

    def near(i):
        return (z + 8 + ((i + 1) // 2) * (2 * (i % 2) - 1)) % 8

    coef[...] = jnp.concatenate([lon_ref[0], lon_ref[1], lat_ref[0], lat_ref[1]], axis=0).T
    rows[:, :, 2 * NLON:, :] = jnp.zeros((2, 8, KPAD - 2 * NLON, B), jnp.bfloat16)

    @pl.when(space == 0)
    def _():
        halo[0] = jnp.zeros((2, NLON, B), jnp.bfloat16)

    @pl.when(space == 15)
    def _():
        halo[1] = jnp.zeros((2, NLON, B), jnp.bfloat16)

    for place, j in enumerate((1, 2, 5, 6)):
        stencil(j, place)

    pl.semaphore_wait(
        barrier,
        20 + (space > 0).astype(jnp.int32) + (space < 15).astype(jnp.int32))

    @pl.when(space < 15)
    def _():
        for f in range(2):
            halo_down(f).start()

    @pl.when(space > 0)
    def _():
        for f in range(2):
            halo_up(f).start()

    @pl.when(core == 0)
    def _():
        for f in range(2):
            halo_up(f).wait_recv()
            stencil(4 * f + 3, 4 + f)

    @pl.when(core == 1)
    def _():
        for f in range(2):
            halo_down(f).wait_recv()
            stencil(4 * f, 4 + f)

    def rest_of_band(n):
        @pl.when(core == 0)
        def _():
            @pl.when(space > 0)
            def _():
                for f in range(2):
                    halo_down(f).wait_recv()

            for f in range(2):
                stencil(4 * f, 6 + f)

        @pl.when(core == 1)
        def _():
            @pl.when(space < 15)
            def _():
                for f in range(2):
                    halo_up(f).wait_recv()

            for f in range(2):
                stencil(4 * f + 3, 6 + f)

    def y_copy(yy, zz, late):
        block = slot(yy, zz, core, late)
        return copy(block, block, y_s.at[late, zz], y_r.at[late, zz], y_dev)

    def c_copy(yy, zz, cc, late):
        block = slot(yy, zz, cc, late)
        return copy(block, block, c_s.at[late, yy, zz], c_r.at[late, yy, zz], c_dev)

    def c_arrive(yy, zz):
        for late in range(2):
            c_copy(yy, zz, 1 - core, late).wait_recv()

    def turn(zz):
        c_arrive(yl, zz)
        a2[blk(zz), :] = rows[yl, zz].T

    def blk(kk):
        return pl.ds(pl.multiple_of(kk * B, B), B)

    def quarter(kk, to):
        return pl.ds(pl.multiple_of(kk * B + to * QT, QT), QT)

    def x_copy(m, kk, dx):
        to = (xx + dx) % 4
        return copy(part.at[m, quarter(kk, to), :], xin.at[m, kk, 3 - dx], x_s.at[m, kk], x_r.at[m, kk],
                    (snap, to * 4 + yh * 2 + core))

    def x_all(m, kk):
        whole = xin.at[m, kk]
        return copy(whole, whole, x_s.at[m, kk], x_r.at[m, kk], (snap, space))

    def z_of(m, kk):
        return (m + 8 - 4 + kk - off) % 8

    def f_start(m, kk, r):
        to, yy = z_of(m, kk), m % 2
        here, there = fin.at[m, kk], zin.at[m // 2, z, yh]

        @pl.when((to == z) & (yy == yh))
        def _():
            pltpu.make_async_copy(here, there, f_r.at[m // 2]).start()

        @pl.when((to != z) | (yy != yh))
        def _():
            copy(here, there, f_s.at[m, kk], f_r.at[m // 2], (to * 2 + yl, xx * 4 + yy * 2 + core)).start()

    def take(n, late):
        zz = near(n)
        if n == 0:
            local_copy(late).wait()
        else:
            block = slot(yl, zz, core, late)
            copy(block, block, z_s.at[late, zz], z_r.at[late, zz], (snap, space)).wait_recv()
        c_copy(yl, zz, core, late).start()

    def share(n, late):
        y_copy(1 - yl, near(n), late).wait_recv()
        c_copy(1 - yl, near(n), core, late).start()

    def pairs(t, use):
        u = near(t)

        def one(n, carry):
            w = near(n)
            k1 = (u + 8 - w - off) % 8
            k2 = (w + 8 - u - off) % 8

            @pl.when(k1 < nb)
            def _():
                use(u, 4 - k1, w)

            @pl.when((n < t) & (k2 < nb))
            def _():
                use(w, 4 - k2, u)

            return carry

        lax.fori_loop(0, t + 1, one, 0)

    def multiply(m, kk, r):
        part[m, blk(kk), :] = jnp.dot(a2[blk(r), :], rows[core, m], preferred_element_type=jnp.float32)

    def send(m, kk, r):
        for dx in range(1, 4):
            x_copy(m, kk, dx).start()

    def add(m, kk, r):
        x_all(m, kk).wait_recv()
        fin[m, kk] = part[m, quarter(kk, xx), :] + xin[m, kk, 0] + xin[m, kk, 1] + xin[m, kk, 2]

    def products(t):
        turn(near(t))
        c_arrive(1 - yl, near(t))
        pairs(t, multiply)
        pairs(t, send)

    def x_sum(t):
        pairs(t, add)
        pairs(t, f_start)

    actions = {"h": rest_of_band, "p": products, "x": x_sum}
    for late, names in enumerate(("lztysw", "LZTYSW")):
        for name, action in zip(names, (
                lambda n, late: local_copy(late).start(),
                lambda n, late: z_copy(near(n), late).start(),
                take,
                lambda n, late: y_copy(yl, near(n), late).start(),
                share,
                lambda n, late: z_copy(near(n), late).wait_send())):
            actions[name] = functools.partial(action, late=late)
    for name, n in ORDER:
        actions[name](n)

    def column(n):
        mx = (xx + n) % 4
        m = 2 * mx + yh
        k = (m + 8 - off - z) % 8
        d = 2 * (k + off) + core - yl
        return mx, m, k < nb, (k < nb) & (d >= 1) & (d <= 7)

    rowq = pl.ds(pl.multiple_of(xx * QT, QT), QT)

    def o_copy(n):
        mx, m, _, _ = column(n)
        return copy(tot.at[mx], obuf.at[rowq, :], o_s.at[mx], o_r, (snap, mx * 4 + yh * 2 + core))

    def m_copy(n):
        mx, m, _, _ = column(n)
        return copy(tot.at[mx], minb.at[rowq, :], m_s.at[mx], m_r, (m * 2 + core, snap))

    for n in (1, 2, 3, 0):
        mx, m, mine, mirrored = column(n)

        @pl.when(mine)
        def _():
            pltpu.make_async_copy(zin.at[mx], zin.at[mx], f_r.at[mx]).wait()
            total = zin[mx, 0, 0]
            for zz in range(8):
                for yy in range(2):
                    if zz + yy:
                        total = total + zin[mx, zz, yy]
            tot[mx] = total

    for n in (1, 2, 3, 0):
        mx, m, mine, mirrored = column(n)

        @pl.when(mirrored)
        def _():
            m_copy(n).start()

        @pl.when(mine)
        def _():
            if n:
                o_copy(n).start()
            else:
                pltpu.make_async_copy(tot.at[mx], obuf.at[rowq, :], o_r).start()

    k_me = (m_me + 8 - off - z) % 8

    @pl.when(k_me < nb)
    def _():
        pltpu.make_async_copy(obuf, obuf, o_r).wait()
        o_ref[...] = obuf[...]

    @pl.when(k_me >= nb)
    def _():
        pltpu.make_async_copy(minb, minb, m_r).wait()
        o_ref[...] = minb[...].T

    @pl.when(space < 15)
    def _():
        for f in range(2):
            halo_down(f).wait_send()

    @pl.when(space > 0)
    def _():
        for f in range(2):
            halo_up(f).wait_send()

    for n in range(1, 8):
        for late in range(2):
            if ("wW"[late], n) not in ORDER:
                z_copy(near(n), late).wait_send()

    def drain(zz, carry):
        for late in range(2):
            y_copy(yl, zz, late).wait_send()
            c_copy(0, zz, core, late).wait_send()
            c_copy(1, zz, core, late).wait_send()
        return carry

    lax.fori_loop(0, 8, drain, 0)

    def drain_blocks(kk, carry):
        def one(m, c):
            x_all(m, kk).wait_send()

            @pl.when((z_of(m, kk) != z) | (m % 2 != yh))
            def _():
                copy(fin.at[m, kk], fin.at[m, kk], f_s.at[m, kk], f_r.at[0], (snap, space)).wait_send()

            return c

        return lax.fori_loop(0, 8, one, carry)

    lax.fori_loop(kk0, 5, drain_blocks, 0)

    for n in range(4):
        mx, m, mine, mirrored = column(n)

        @pl.when(mirrored)
        def _():
            m_copy(n).wait_send()

        if n:
            @pl.when(mine)
            def _():
                o_copy(n).wait_send()


def shards(factors, snapshots, lon_coeff, lat_coeff):
    x = jnp.transpose(snapshots, (1, 2, 3, 0)).reshape(8, NLON, B)
    dma = pltpu.SemaphoreType.DMA
    vmem = pl.BlockSpec(memory_space=pltpu.VMEM)
    bf, f32 = jnp.bfloat16, jnp.float32
    return pl.pallas_call(
        kernel,
        out_shape=jax.ShapeDtypeStruct((B, B), f32),
        in_specs=[vmem, vmem, vmem, pl.BlockSpec(memory_space=pltpu.SMEM)],
        out_specs=vmem,
        scratch_shapes=[
            pltpu.VMEM((NLON, 16), f32),
            pltpu.VMEM((2, 2, NLON, B), bf),
            pltpu.VMEM((8, NLON + 16, B), f32),
            pltpu.VMEM((8 * NLON, B), bf),
            pltpu.VMEM((2, 8, KPAD, B), bf),
            pltpu.VMEM((8 * B, KPAD), bf),
            pltpu.VMEM((8, 5 * B, B), f32),
            pltpu.VMEM((8, 5, 3, QT, B), f32),
            pltpu.VMEM((8, 5, QT, B), f32),
            pltpu.VMEM((4, 8, 2, QT, B), f32),
            pltpu.VMEM((4, QT, B), f32),
            pltpu.VMEM((B, B), f32),
            pltpu.VMEM((B, B), f32),
            dma((2, 2)), dma((2, 2)), dma((2,)),
            dma((2, 8)), dma((2, 8)),
            dma((2, 8)), dma((2, 8)),
            dma((2, 2, 8)), dma((2, 2, 8)),
            dma((8, 5)), dma((8, 5)),
            dma((8, 5)), dma((4,)),
            dma((4,)), dma, dma((4,)), dma,
        ],
        compiler_params=pltpu.CompilerParams(collective_id=0, has_side_effects=True),
        name="gram",
    )(x, lon_coeff, lat_coeff, jnp.asarray(factors))


def solution(mesh):
    factors = row_factors(2, 64, NLON)
    return jax.shard_map(
        functools.partial(shards, factors),
        mesh=mesh,
        in_specs=(P("snap", None, "space", None), P(None, "space", None), P(None, "space", None)),
        out_specs=P("snap", "space"),
        check_vma=False,
    )
```

```python
import functools
import math

import jax
import jax.numpy as jnp
import numpy as np
from jax import lax
from jax.experimental import pallas as pl
from jax.experimental.pallas import tpu as pltpu
from jax.sharding import PartitionSpec as P

MESH = pl.DeviceIdType.MESH
NLON = 720
KPAD = 1536
B = 128
CH = 144
QT = B // 4
EARLY, LATE = 528, 192
ORDER = [(word[:1], int(word[1:])) for word in (
    "l0", "z1", "z2", "t0", "y0", "w1", "w2", "z3", "z4", "t1", "y1", "t2", "s0", "y2", "w3", "w4", "z5", "z6",
    "h0", "L0", "Z1", "Z2", "Z3", "Z4", "Z5", "Z6", "T0", "Y0", "t3", "s1", "y3", "t4", "s2", "y4", "z7", "Z7",
    "S0", "T1", "Y1", "T2", "Y2", "p0", "s3", "S1", "p1", "S2", "p2", "T3", "Y3", "T4", "Y4", "x0", "t5", "y5",
    "t6", "y6", "s4", "S3", "p3", "x1", "S4", "p4", "x2", "T5", "Y5", "T6", "Y6", "T7", "t7", "y7", "Y7", "s5",
    "S5", "p5", "x3", "s6", "S6", "p6", "x4", "s7", "S7", "p7", "x5", "x6", "x7",
)]


def row_factors(fields, nlat, nlon):
    lat = (45.0 + 0.5 * (np.arange(nlat) + 0.5 - nlat / 2.0)) * (math.pi / 180.0)
    cosine = np.cos(lat)
    total = fields * nlon * cosine.sum()
    return (np.sqrt(cosine) * total ** (-0.25)).astype(np.float32)


def kernel(x_hbm, lon_ref, lat_ref, fac_ref, o_ref,
           x_ref, coef, halo, v32, sc, rows, a2, part, xin, fin, zin, tot, obuf, minb,
           load_s, halo_s, halo_r, loc_s, z_s, z_r, y_s, y_r, c_s, c_r, x_s, x_r, f_s, f_r,
           o_s, o_r, m_s, m_r):
    snap = lax.axis_index("snap")
    space = lax.axis_index("space")
    z, yl = snap // 2, snap % 2
    xx, yh, core = space // 4, (space // 2) % 2, space % 2
    m_me = space // 2
    same = (core == yl).astype(jnp.int32)
    nb = 4 + same
    kk0 = 1 - same
    off = jnp.where(same == 1, 0, yl)

    def load(j):
        return pltpu.make_async_copy(x_hbm.at[j], x_ref.at[j], load_s.at[j])

    for j in (1, 2, 0, 3, 5, 6, 4, 7):
        load(j).start()

    def copy(src, dst, ss, rs, dev):
        return pltpu.make_async_remote_copy(
            src_ref=src, dst_ref=dst, send_sem=ss, recv_sem=rs, device_id=dev, device_id_type=MESH)

    up_dev = (snap, jnp.maximum(space - 1, 0))
    dn_dev = (snap, jnp.minimum(space + 1, 15))
    y_dev = (z * 2 + 1 - yl, space)
    c_dev = (snap, m_me * 2 + 1 - core)
    h_dev = (snap, xx * 4 + (1 - yh) * 2 + core)

    barrier = pltpu.get_barrier_semaphore()

    def greet(dev):
        pl.semaphore_signal(barrier, inc=1, device_id=dev, device_id_type=MESH)

    for dz in (1, 2, 6, 7):
        greet((((z + dz) % 8) * 2 + yl, space))
    for dx in range(1, 4):
        greet((snap, ((xx + dx) % 4) * 4 + yh * 2 + core))
    greet(y_dev)
    greet(c_dev)
    greet(h_dev)

    @pl.when(space > 0)
    def _():
        greet(up_dev)

    @pl.when(space < 15)
    def _():
        greet(dn_dev)

    def halo_down(f):
        return copy(x_hbm.at[4 * f + 3], halo.at[0, f], halo_s.at[0, f], halo_r.at[0, f], dn_dev)

    def halo_up(f):
        return copy(x_hbm.at[4 * f], halo.at[1, f], halo_s.at[1, f], halo_r.at[1, f], up_dev)

    def span(late):
        return LATE if late else EARLY

    def slot(yy, zz, cc, late):
        return rows.at[yy, zz, pl.ds(pl.multiple_of(cc * NLON + late * EARLY, 16), span(late)), :]

    def stencil(j, place):
        f, row = divmod(j, 4)
        v = x_ref[j].astype(jnp.float32)
        v32[j, pl.ds(8, NLON), :] = v
        v32[j, 7:8, :] = v[NLON - 1:, :]
        v32[j, NLON + 8:NLON + 9, :] = v[:1, :]
        scale = fac_ref[space * 4 + row]
        for s in range(0, NLON, CH):
            a = v32[j, pl.ds(8 + s, CH), :]
            west = v32[j, pl.ds(7 + s, CH), :]
            east = v32[j, pl.ds(9 + s, CH), :]
            if row == 0:
                north = halo[0, f, pl.ds(s, CH), :]
            else:
                north = x_ref[j - 1, pl.ds(s, CH), :]
            if row == 3:
                south = halo[1, f, pl.ds(s, CH), :]
            else:
                south = x_ref[j + 1, pl.ds(s, CH), :]
            lon_part = west + east - 2.0 * a
            lat_part = south.astype(jnp.float32) + north.astype(jnp.float32) - 2.0 * a
            smooth = a + coef[pl.ds(s, CH), j:j + 1] * lon_part + coef[pl.ds(s, CH), 8 + j:9 + j] * lat_part
            sc[pl.ds(place * NLON + s, CH), :] = (smooth * scale).astype(jnp.bfloat16)

    def mine_for(zz, late):
        return sc.at[pl.ds(pl.multiple_of(late * 8 * EARLY + zz * span(late), 16), span(late)), :]

    def z_copy(zz, late):
        return copy(mine_for(zz, late), slot(yl, z, core, late), z_s.at[late, zz], z_r.at[late, z],
                    (zz * 2 + yl, space))

    def local_copy(late):
        return pltpu.make_async_copy(mine_for(z, late), slot(yl, z, core, late), loc_s.at[late])

    def near(i):
        return (z + 8 + ((i + 1) // 2) * (2 * (i % 2) - 1)) % 8

    coef[...] = jnp.concatenate([lon_ref[0], lon_ref[1], lat_ref[0], lat_ref[1]], axis=0).T
    rows[:, :, 2 * NLON:, :] = jnp.zeros((2, 8, KPAD - 2 * NLON, B), jnp.bfloat16)

    @pl.when(space == 0)
    def _():
        halo[0] = jnp.zeros((2, NLON, B), jnp.bfloat16)

    @pl.when(space == 15)
    def _():
        halo[1] = jnp.zeros((2, NLON, B), jnp.bfloat16)

    for j in (1, 2, 0, 3):
        load(j).wait()
    stencil(1, 0)
    stencil(2, 1)
    for j in (5, 6, 4, 7):
        load(j).wait()
    stencil(5, 2)
    stencil(6, 3)

    pl.semaphore_wait(
        barrier,
        10 + (space > 0).astype(jnp.int32) + (space < 15).astype(jnp.int32))

    @pl.when(space < 15)
    def _():
        for f in range(2):
            halo_down(f).start()

    @pl.when(space > 0)
    def _():
        for f in range(2):
            halo_up(f).start()

    @pl.when(core == 0)
    def _():
        for f in range(2):
            halo_up(f).wait_recv()
            stencil(4 * f + 3, 4 + f)

    @pl.when(core == 1)
    def _():
        for f in range(2):
            halo_down(f).wait_recv()
            stencil(4 * f, 4 + f)

    def rest_of_band(n):
        @pl.when(core == 0)
        def _():
            @pl.when(space > 0)
            def _():
                for f in range(2):
                    halo_down(f).wait_recv()

            for f in range(2):
                stencil(4 * f, 6 + f)

        @pl.when(core == 1)
        def _():
            @pl.when(space < 15)
            def _():
                for f in range(2):
                    halo_up(f).wait_recv()

            for f in range(2):
                stencil(4 * f + 3, 6 + f)

    def y_copy(yy, zz, late):
        block = slot(yy, zz, core, late)
        return copy(block, block, y_s.at[late, zz], y_r.at[late, zz], y_dev)

    def c_copy(yy, zz, cc, late):
        block = slot(yy, zz, cc, late)
        return copy(block, block, c_s.at[late, yy, zz], c_r.at[late, yy, zz], c_dev)

    def c_arrive(yy, zz):
        for late in range(2):
            c_copy(yy, zz, 1 - core, late).wait_recv()

    def turn(zz):
        c_arrive(yl, zz)
        a2[blk(zz), :] = rows[yl, zz].T

    def blk(kk):
        return pl.ds(pl.multiple_of(kk * B, B), B)

    def quarter(kk, to):
        return pl.ds(pl.multiple_of(kk * B + to * QT, QT), QT)

    def x_copy(m, kk, dx):
        to = (xx + dx) % 4
        return copy(part.at[m, quarter(kk, to), :], xin.at[m, kk, 3 - dx], x_s.at[m, kk], x_r.at[m, kk],
                    (snap, to * 4 + yh * 2 + core))

    def x_all(m, kk):
        whole = xin.at[m, kk]
        return copy(whole, whole, x_s.at[m, kk], x_r.at[m, kk], (snap, space))

    def z_of(m, kk):
        return (m + 8 - 4 + kk - off) % 8

    def f_start(m, kk, r):
        to, yy = z_of(m, kk), m % 2
        here, there = fin.at[m, kk], zin.at[m // 2, z, yh]

        @pl.when((to == z) & (yy == yh))
        def _():
            pltpu.make_async_copy(here, there, f_r.at[m // 2]).start()

        @pl.when((to != z) | (yy != yh))
        def _():
            copy(here, there, f_s.at[m, kk], f_r.at[m // 2], (to * 2 + yl, xx * 4 + yy * 2 + core)).start()

    def take(n, late):
        zz = near(n)
        if n == 0:
            local_copy(late).wait()
        else:
            block = slot(yl, zz, core, late)
            copy(block, block, z_s.at[late, zz], z_r.at[late, zz], (snap, space)).wait_recv()
        c_copy(yl, zz, core, late).start()

    def share(n, late):
        y_copy(1 - yl, near(n), late).wait_recv()
        c_copy(1 - yl, near(n), core, late).start()

    def pairs(t, use, then):
        u = near(t)

        def each(n, what):
            w = near(n)
            k1 = (u + 8 - w - off) % 8
            k2 = (w + 8 - u - off) % 8

            @pl.when(k1 < nb)
            def _():
                what(u, 4 - k1, w)

            @pl.when((n < t) & (k2 < nb))
            def _():
                what(w, 4 - k2, u)

        def one(n, carry):
            each(n, use)

            @pl.when(n > 0)
            def _():
                each(n - 1, then)

            return carry

        lax.fori_loop(0, t + 1, one, 0)
        each(t, then)

    def multiply(m, kk, r):
        part[m, blk(kk), :] = jnp.dot(a2[blk(r), :], rows[core, m], preferred_element_type=jnp.float32)

    def send(m, kk, r):
        for dx in range(1, 4):
            x_copy(m, kk, dx).start()

    def add(m, kk, r):
        x_all(m, kk).wait_recv()
        fin[m, kk] = part[m, quarter(kk, xx), :] + xin[m, kk, 0] + xin[m, kk, 1] + xin[m, kk, 2]

    def products(t):
        turn(near(t))
        c_arrive(1 - yl, near(t))
        pairs(t, multiply, send)

    def x_sum(t):
        pairs(t, add, f_start)

    actions = {"h": rest_of_band, "p": products, "x": x_sum}
    for late, names in enumerate(("lztysw", "LZTYSW")):
        for name, action in zip(names, (
                lambda n, late: local_copy(late).start(),
                lambda n, late: z_copy(near(n), late).start(),
                take,
                lambda n, late: y_copy(yl, near(n), late).start(),
                share,
                lambda n, late: z_copy(near(n), late).wait_send())):
            actions[name] = functools.partial(action, late=late)
    for name, n in ORDER:
        actions[name](n)

    @pl.when(space < 15)
    def _():
        for f in range(2):
            halo_down(f).wait_send()

    @pl.when(space > 0)
    def _():
        for f in range(2):
            halo_up(f).wait_send()

    for n in range(1, 8):
        for late in range(2):
            if ("wW"[late], n) not in ORDER:
                z_copy(near(n), late).wait_send()

    def drain(zz, carry):
        for late in range(2):
            y_copy(yl, zz, late).wait_send()
            c_copy(0, zz, core, late).wait_send()
            c_copy(1, zz, core, late).wait_send()
        return carry

    lax.fori_loop(0, 8, drain, 0)

    def x_over(kk, carry):
        def one(m, c):
            x_all(m, kk).wait_send()
            return c

        return lax.fori_loop(0, 8, one, carry)

    lax.fori_loop(kk0, 5, x_over, 0)

    def column(n):
        mx = (xx + n) % 4
        m = 2 * mx + yh
        k = (m + 8 - off - z) % 8
        d = 2 * (k + off) + core - yl
        return mx, m, k < nb, (k < nb) & (d >= 1) & (d <= 7)

    rowq = pl.ds(pl.multiple_of(xx * QT, QT), QT)

    def o_copy(n):
        mx, m, _, _ = column(n)
        return copy(tot.at[mx], obuf.at[rowq, :], o_s.at[mx], o_r, (snap, mx * 4 + yh * 2 + core))

    def m_copy(n):
        mx, m, _, _ = column(n)
        return copy(tot.at[mx], minb.at[rowq, :], m_s.at[mx], m_r, (m * 2 + core, snap))

    def whole(n):
        mx, m, mine, mirrored = column(n)

        @pl.when(mine)
        def _():
            pltpu.make_async_copy(zin.at[mx], zin.at[mx], f_r.at[mx]).wait()
            total = zin[mx, 0, 0]
            for zz in range(8):
                for yy in range(2):
                    if zz + yy:
                        total = total + zin[mx, zz, yy]
            tot[mx] = total

    def place(n):
        mx, m, mine, mirrored = column(n)

        @pl.when(mirrored)
        def _():
            m_copy(n).start()

        @pl.when(mine)
        def _():
            if n:
                o_copy(n).start()
            else:
                pltpu.make_async_copy(tot.at[mx], obuf.at[rowq, :], o_r).start()

    whole(2)
    whole(1)
    place(2)
    whole(3)
    place(1)
    whole(0)
    place(3)
    place(0)

    def f_over(kk, carry):
        def one(m, c):
            @pl.when((z_of(m, kk) != z) | (m % 2 != yh))
            def _():
                copy(fin.at[m, kk], fin.at[m, kk], f_s.at[m, kk], f_r.at[0], (snap, space)).wait_send()

            return c

        return lax.fori_loop(0, 8, one, carry)

    lax.fori_loop(kk0, 5, f_over, 0)

    for n in range(4):
        mx, m, mine, mirrored = column(n)

        @pl.when(mirrored)
        def _():
            m_copy(n).wait_send()

        if n:
            @pl.when(mine)
            def _():
                o_copy(n).wait_send()

    k_me = (m_me + 8 - off - z) % 8

    @pl.when(k_me < nb)
    def _():
        pltpu.make_async_copy(obuf, obuf, o_r).wait()
        o_ref[...] = obuf[...]

    @pl.when(k_me >= nb)
    def _():
        pltpu.make_async_copy(minb, minb, m_r).wait()
        o_ref[...] = minb[...].T


def shards(factors, snapshots, lon_coeff, lat_coeff):
    x = jnp.transpose(snapshots, (1, 2, 3, 0)).reshape(8, NLON, B)
    dma = pltpu.SemaphoreType.DMA
    vmem = pl.BlockSpec(memory_space=pltpu.VMEM)
    bf, f32 = jnp.bfloat16, jnp.float32
    return pl.pallas_call(
        kernel,
        out_shape=jax.ShapeDtypeStruct((B, B), f32),
        in_specs=[pl.BlockSpec(memory_space=pl.ANY), vmem, vmem, pl.BlockSpec(memory_space=pltpu.SMEM)],
        out_specs=vmem,
        scratch_shapes=[
            pltpu.VMEM((8, NLON, B), bf),
            pltpu.VMEM((NLON, 16), f32),
            pltpu.VMEM((2, 2, NLON, B), bf),
            pltpu.VMEM((8, NLON + 16, B), f32),
            pltpu.VMEM((8 * NLON, B), bf),
            pltpu.VMEM((2, 8, KPAD, B), bf),
            pltpu.VMEM((8 * B, KPAD), bf),
            pltpu.VMEM((8, 5 * B, B), f32),
            pltpu.VMEM((8, 5, 3, QT, B), f32),
            pltpu.VMEM((8, 5, QT, B), f32),
            pltpu.VMEM((4, 8, 2, QT, B), f32),
            pltpu.VMEM((4, QT, B), f32),
            pltpu.VMEM((B, B), f32),
            pltpu.VMEM((B, B), f32),
            dma((8,)), dma((2, 2)), dma((2, 2)), dma((2,)),
            dma((2, 8)), dma((2, 8)),
            dma((2, 8)), dma((2, 8)),
            dma((2, 2, 8)), dma((2, 2, 8)),
            dma((8, 5)), dma((8, 5)),
            dma((8, 5)), dma((4,)),
            dma((4,)), dma, dma((4,)), dma,
        ],
        compiler_params=pltpu.CompilerParams(collective_id=0, has_side_effects=True),
        name="gram",
    )(x, lon_coeff, lat_coeff, jnp.asarray(factors))


def solution(mesh):
    factors = row_factors(2, 64, NLON)
    return jax.shard_map(
        functools.partial(shards, factors),
        mesh=mesh,
        in_specs=(P("snap", None, "space", None), P(None, "space", None), P(None, "space", None)),
        out_specs=P("snap", "space"),
        check_vma=False,
    )
```

```python
import functools
import math

import jax
import jax.numpy as jnp
import numpy as np
from jax import lax
from jax.experimental import pallas as pl
from jax.experimental.pallas import tpu as pltpu
from jax.sharding import PartitionSpec as P

MESH = pl.DeviceIdType.MESH
NLON = 720
KPAD = 1536
B = 128
CH = 144
QT = B // 4
EARLY, LATE = 528, 192
ORDER = [(word[:1], int(word[1:])) for word in (
    "l0", "z1", "z2", "t0", "y0", "w1", "z3", "w2", "z4", "t1", "y1", "t2", "s0", "y2", "h0", "L0", "Z1", "Z2",
    "Z3", "Z4", "w3", "z5", "w4", "z6", "Z5", "Z6", "T0", "Y0", "t3", "s1", "y3", "t4", "s2", "y4", "z7", "Z7",
    "S0", "T1", "Y1", "T2", "Y2", "p0", "s3", "S1", "p1", "S2", "p2", "T3", "Y3", "T4", "Y4", "T5", "Y5", "T6",
    "Y6", "x0", "t5", "y5", "t6", "y6", "s4", "S3", "p3", "x1", "S4", "p4", "x2", "T7", "Y7", "t7", "y7", "s5",
    "S5", "p5", "x3", "S6", "s6", "p6", "x4", "S7", "s7", "p7", "x5", "x6", "x7",
)]


def row_factors(fields, nlat, nlon):
    lat = (45.0 + 0.5 * (np.arange(nlat) + 0.5 - nlat / 2.0)) * (math.pi / 180.0)
    cosine = np.cos(lat)
    total = fields * nlon * cosine.sum()
    return (np.sqrt(cosine) * total ** (-0.25)).astype(np.float32)


def kernel(x_hbm, lon_ref, lat_ref, fac_ref, o_ref,
           x_ref, coef, halo, v32, sc, rows, a2, part, xin, fin, zin, tot, obuf, minb,
           load_s, halo_s, halo_r, loc_s, z_s, z_r, y_s, y_r, c_s, c_r, x_s, x_r, f_s, f_r,
           o_s, o_r, m_s, m_r):
    snap = lax.axis_index("snap")
    space = lax.axis_index("space")
    z, yl = snap // 2, snap % 2
    xx, yh, core = space // 4, (space // 2) % 2, space % 2
    m_me = space // 2
    same = (core == yl).astype(jnp.int32)
    nb = 4 + same
    kk0 = 1 - same
    off = jnp.where(same == 1, 0, yl)

    def load(j):
        return pltpu.make_async_copy(x_hbm.at[j], x_ref.at[j], load_s.at[j])

    for j in (1, 2, 0, 3, 5, 6, 4, 7):
        load(j).start()

    def copy(src, dst, ss, rs, dev):
        return pltpu.make_async_remote_copy(
            src_ref=src, dst_ref=dst, send_sem=ss, recv_sem=rs, device_id=dev, device_id_type=MESH)

    up_dev = (snap, jnp.maximum(space - 1, 0))
    dn_dev = (snap, jnp.minimum(space + 1, 15))
    y_dev = (z * 2 + 1 - yl, space)
    c_dev = (snap, m_me * 2 + 1 - core)
    h_dev = (snap, xx * 4 + (1 - yh) * 2 + core)

    barrier = pltpu.get_barrier_semaphore()

    def greet(dev):
        pl.semaphore_signal(barrier, inc=1, device_id=dev, device_id_type=MESH)

    for dz in (1, 2, 6, 7):
        greet((((z + dz) % 8) * 2 + yl, space))
    for dx in range(1, 4):
        greet((snap, ((xx + dx) % 4) * 4 + yh * 2 + core))
    greet(y_dev)
    greet(c_dev)
    greet(h_dev)

    @pl.when(space > 0)
    def _():
        greet(up_dev)

    @pl.when(space < 15)
    def _():
        greet(dn_dev)

    def halo_down(f):
        return copy(x_hbm.at[4 * f + 3], halo.at[0, f], halo_s.at[0, f], halo_r.at[0, f], dn_dev)

    def halo_up(f):
        return copy(x_hbm.at[4 * f], halo.at[1, f], halo_s.at[1, f], halo_r.at[1, f], up_dev)

    def span(late):
        return LATE if late else EARLY

    def slot(yy, zz, cc, late):
        return rows.at[yy, zz, pl.ds(pl.multiple_of(cc * NLON + late * EARLY, 16), span(late)), :]

    def stencil(j, place):
        f, row = divmod(j, 4)
        v = x_ref[j].astype(jnp.float32)
        v32[j, pl.ds(8, NLON), :] = v
        v32[j, 7:8, :] = v[NLON - 1:, :]
        v32[j, NLON + 8:NLON + 9, :] = v[:1, :]
        scale = fac_ref[space * 4 + row]
        for s in range(0, NLON, CH):
            a = v32[j, pl.ds(8 + s, CH), :]
            west = v32[j, pl.ds(7 + s, CH), :]
            east = v32[j, pl.ds(9 + s, CH), :]
            if row == 0:
                north = halo[0, f, pl.ds(s, CH), :]
            else:
                north = x_ref[j - 1, pl.ds(s, CH), :]
            if row == 3:
                south = halo[1, f, pl.ds(s, CH), :]
            else:
                south = x_ref[j + 1, pl.ds(s, CH), :]
            lon_part = west + east - 2.0 * a
            lat_part = south.astype(jnp.float32) + north.astype(jnp.float32) - 2.0 * a
            smooth = a + coef[pl.ds(s, CH), j:j + 1] * lon_part + coef[pl.ds(s, CH), 8 + j:9 + j] * lat_part
            sc[pl.ds(place * NLON + s, CH), :] = (smooth * scale).astype(jnp.bfloat16)

    def mine_for(zz, late):
        return sc.at[pl.ds(pl.multiple_of(late * 8 * EARLY + zz * span(late), 16), span(late)), :]

    def z_copy(zz, late):
        return copy(mine_for(zz, late), slot(yl, z, core, late), z_s.at[late, zz], z_r.at[late, z],
                    (zz * 2 + yl, space))

    def local_copy(late):
        return pltpu.make_async_copy(mine_for(z, late), slot(yl, z, core, late), loc_s.at[late])

    def near(i):
        return (z + 8 + ((i + 1) // 2) * (2 * (i % 2) - 1)) % 8

    coef[...] = jnp.concatenate([lon_ref[0], lon_ref[1], lat_ref[0], lat_ref[1]], axis=0).T
    rows[:, :, 2 * NLON:, :] = jnp.zeros((2, 8, KPAD - 2 * NLON, B), jnp.bfloat16)

    @pl.when(space == 0)
    def _():
        halo[0] = jnp.zeros((2, NLON, B), jnp.bfloat16)

    @pl.when(space == 15)
    def _():
        halo[1] = jnp.zeros((2, NLON, B), jnp.bfloat16)

    for j in (1, 2, 0, 3):
        load(j).wait()
    stencil(1, 0)
    stencil(2, 1)
    for j in (5, 6, 4, 7):
        load(j).wait()
    stencil(5, 2)
    stencil(6, 3)

    pl.semaphore_wait(
        barrier,
        10 + (space > 0).astype(jnp.int32) + (space < 15).astype(jnp.int32))

    @pl.when(space < 15)
    def _():
        for f in range(2):
            halo_down(f).start()

    @pl.when(space > 0)
    def _():
        for f in range(2):
            halo_up(f).start()

    @pl.when(core == 0)
    def _():
        for f in range(2):
            halo_up(f).wait_recv()
            stencil(4 * f + 3, 4 + f)

    @pl.when(core == 1)
    def _():
        for f in range(2):
            halo_down(f).wait_recv()
            stencil(4 * f, 4 + f)

    def rest_of_band(n):
        @pl.when(core == 0)
        def _():
            @pl.when(space > 0)
            def _():
                for f in range(2):
                    halo_down(f).wait_recv()

            for f in range(2):
                stencil(4 * f, 6 + f)

        @pl.when(core == 1)
        def _():
            @pl.when(space < 15)
            def _():
                for f in range(2):
                    halo_up(f).wait_recv()

            for f in range(2):
                stencil(4 * f + 3, 6 + f)

    def y_copy(yy, zz, late):
        block = slot(yy, zz, core, late)
        return copy(block, block, y_s.at[late, zz], y_r.at[late, zz], y_dev)

    def c_copy(yy, zz, cc, late):
        block = slot(yy, zz, cc, late)
        return copy(block, block, c_s.at[late, yy, zz], c_r.at[late, yy, zz], c_dev)

    def c_arrive(yy, zz):
        for late in range(2):
            c_copy(yy, zz, 1 - core, late).wait_recv()

    def turn(zz):
        c_arrive(yl, zz)
        a2[blk(zz), :] = rows[yl, zz].T

    def blk(kk):
        return pl.ds(pl.multiple_of(kk * B, B), B)

    def quarter(kk, to):
        return pl.ds(pl.multiple_of(kk * B + to * QT, QT), QT)

    def x_copy(m, kk, dx):
        to = (xx + dx) % 4
        return copy(part.at[m, quarter(kk, to), :], xin.at[m, kk, 3 - dx], x_s.at[m, kk], x_r.at[m, kk],
                    (snap, to * 4 + yh * 2 + core))

    def x_all(m, kk):
        whole = xin.at[m, kk]
        return copy(whole, whole, x_s.at[m, kk], x_r.at[m, kk], (snap, space))

    def z_of(m, kk):
        return (m + 8 - 4 + kk - off) % 8

    def f_start(m, kk, r):
        to, yy = z_of(m, kk), m % 2
        here, there = fin.at[m, kk], zin.at[m // 2, z, yh]

        @pl.when((to == z) & (yy == yh))
        def _():
            pltpu.make_async_copy(here, there, f_r.at[m // 2]).start()

        @pl.when((to != z) | (yy != yh))
        def _():
            copy(here, there, f_s.at[m, kk], f_r.at[m // 2], (to * 2 + yl, xx * 4 + yy * 2 + core)).start()

    def take(n, late):
        zz = near(n)
        if n == 0:
            local_copy(late).wait()
        else:
            block = slot(yl, zz, core, late)
            copy(block, block, z_s.at[late, zz], z_r.at[late, zz], (snap, space)).wait_recv()
        c_copy(yl, zz, core, late).start()

    def share(n, late):
        y_copy(1 - yl, near(n), late).wait_recv()
        c_copy(1 - yl, near(n), core, late).start()

    def pairs(t, use, then):
        u = near(t)

        def each(n, what):
            w = near(n)
            k1 = (u + 8 - w - off) % 8
            k2 = (w + 8 - u - off) % 8

            @pl.when(k1 < nb)
            def _():
                what(u, 4 - k1, w)

            @pl.when((n < t) & (k2 < nb))
            def _():
                what(w, 4 - k2, u)

        def one(n, carry):
            each(n, use)

            @pl.when(n > 0)
            def _():
                each(n - 1, then)

            return carry

        lax.fori_loop(0, t + 1, one, 0)
        each(t, then)

    def multiply(m, kk, r):
        part[m, blk(kk), :] = jnp.dot(a2[blk(r), :], rows[core, m], preferred_element_type=jnp.float32)

    def send(m, kk, r):
        for dx in range(1, 4):
            x_copy(m, kk, dx).start()

    def add(m, kk, r):
        x_all(m, kk).wait_recv()
        fin[m, kk] = part[m, quarter(kk, xx), :] + xin[m, kk, 0] + xin[m, kk, 1] + xin[m, kk, 2]

    def products(t):
        turn(near(t))
        c_arrive(1 - yl, near(t))
        pairs(t, multiply, send)

    def x_sum(t):
        pairs(t, add, f_start)

    actions = {"h": rest_of_band, "p": products, "x": x_sum}
    for late, names in enumerate(("lztysw", "LZTYSW")):
        for name, action in zip(names, (
                lambda n, late: local_copy(late).start(),
                lambda n, late: z_copy(near(n), late).start(),
                take,
                lambda n, late: y_copy(yl, near(n), late).start(),
                share,
                lambda n, late: z_copy(near(n), late).wait_send())):
            actions[name] = functools.partial(action, late=late)
    for name, n in ORDER:
        actions[name](n)

    @pl.when(space < 15)
    def _():
        for f in range(2):
            halo_down(f).wait_send()

    @pl.when(space > 0)
    def _():
        for f in range(2):
            halo_up(f).wait_send()

    for n in range(1, 8):
        for late in range(2):
            if ("wW"[late], n) not in ORDER:
                z_copy(near(n), late).wait_send()

    def drain(zz, carry):
        for late in range(2):
            y_copy(yl, zz, late).wait_send()
            c_copy(0, zz, core, late).wait_send()
            c_copy(1, zz, core, late).wait_send()
        return carry

    lax.fori_loop(0, 8, drain, 0)

    def x_over(kk, carry):
        def one(m, c):
            x_all(m, kk).wait_send()
            return c

        return lax.fori_loop(0, 8, one, carry)

    lax.fori_loop(kk0, 5, x_over, 0)

    def column(n):
        mx = (xx + n) % 4
        m = 2 * mx + yh
        k = (m + 8 - off - z) % 8
        d = 2 * (k + off) + core - yl
        return mx, m, k < nb, (k < nb) & (d >= 1) & (d <= 7)

    rowq = pl.ds(pl.multiple_of(xx * QT, QT), QT)

    def o_copy(n):
        mx, m, _, _ = column(n)
        return copy(tot.at[mx], obuf.at[rowq, :], o_s.at[mx], o_r, (snap, mx * 4 + yh * 2 + core))

    def m_copy(n):
        mx, m, _, _ = column(n)
        return copy(tot.at[mx], minb.at[rowq, :], m_s.at[mx], m_r, (m * 2 + core, snap))

    def whole(n):
        mx, m, mine, mirrored = column(n)

        @pl.when(mine)
        def _():
            pltpu.make_async_copy(zin.at[mx], zin.at[mx], f_r.at[mx]).wait()
            total = zin[mx, 0, 0]
            for zz in range(8):
                for yy in range(2):
                    if zz + yy:
                        total = total + zin[mx, zz, yy]
            tot[mx] = total

    def place(n):
        mx, m, mine, mirrored = column(n)

        @pl.when(mirrored)
        def _():
            m_copy(n).start()

        @pl.when(mine)
        def _():
            if n:
                o_copy(n).start()
            else:
                pltpu.make_async_copy(tot.at[mx], obuf.at[rowq, :], o_r).start()

    whole(2)
    whole(1)
    place(2)
    whole(3)
    place(1)
    whole(0)
    place(3)
    place(0)

    def f_over(kk, carry):
        def one(m, c):
            @pl.when((z_of(m, kk) != z) | (m % 2 != yh))
            def _():
                copy(fin.at[m, kk], fin.at[m, kk], f_s.at[m, kk], f_r.at[0], (snap, space)).wait_send()

            return c

        return lax.fori_loop(0, 8, one, carry)

    lax.fori_loop(kk0, 5, f_over, 0)

    for n in range(4):
        mx, m, mine, mirrored = column(n)

        @pl.when(mirrored)
        def _():
            m_copy(n).wait_send()

        if n:
            @pl.when(mine)
            def _():
                o_copy(n).wait_send()

    k_me = (m_me + 8 - off - z) % 8

    @pl.when(k_me < nb)
    def _():
        pltpu.make_async_copy(obuf, obuf, o_r).wait()
        o_ref[...] = obuf[...]

    @pl.when(k_me >= nb)
    def _():
        pltpu.make_async_copy(minb, minb, m_r).wait()
        o_ref[...] = minb[...].T


def shards(factors, snapshots, lon_coeff, lat_coeff):
    x = jnp.transpose(snapshots, (1, 2, 3, 0)).reshape(8, NLON, B)
    dma = pltpu.SemaphoreType.DMA
    vmem = pl.BlockSpec(memory_space=pltpu.VMEM)
    bf, f32 = jnp.bfloat16, jnp.float32
    return pl.pallas_call(
        kernel,
        out_shape=jax.ShapeDtypeStruct((B, B), f32),
        in_specs=[pl.BlockSpec(memory_space=pl.ANY), vmem, vmem, pl.BlockSpec(memory_space=pltpu.SMEM)],
        out_specs=vmem,
        scratch_shapes=[
            pltpu.VMEM((8, NLON, B), bf),
            pltpu.VMEM((NLON, 16), f32),
            pltpu.VMEM((2, 2, NLON, B), bf),
            pltpu.VMEM((8, NLON + 16, B), f32),
            pltpu.VMEM((8 * NLON, B), bf),
            pltpu.VMEM((2, 8, KPAD, B), bf),
            pltpu.VMEM((8 * B, KPAD), bf),
            pltpu.VMEM((8, 5 * B, B), f32),
            pltpu.VMEM((8, 5, 3, QT, B), f32),
            pltpu.VMEM((8, 5, QT, B), f32),
            pltpu.VMEM((4, 8, 2, QT, B), f32),
            pltpu.VMEM((4, QT, B), f32),
            pltpu.VMEM((B, B), f32),
            pltpu.VMEM((B, B), f32),
            dma((8,)), dma((2, 2)), dma((2, 2)), dma((2,)),
            dma((2, 8)), dma((2, 8)),
            dma((2, 8)), dma((2, 8)),
            dma((2, 2, 8)), dma((2, 2, 8)),
            dma((8, 5)), dma((8, 5)),
            dma((8, 5)), dma((4,)),
            dma((4,)), dma, dma((4,)), dma,
        ],
        compiler_params=pltpu.CompilerParams(collective_id=0, has_side_effects=True),
        name="gram",
    )(x, lon_coeff, lat_coeff, jnp.asarray(factors))


def solution(mesh):
    factors = row_factors(2, 64, NLON)
    return jax.shard_map(
        functools.partial(shards, factors),
        mesh=mesh,
        in_specs=(P("snap", None, "space", None), P(None, "space", None), P(None, "space", None)),
        out_specs=P("snap", "space"),
        check_vma=False,
    )
```

```python
import functools
import math

import jax
import jax.numpy as jnp
import numpy as np
from jax import lax
from jax.experimental import pallas as pl
from jax.experimental.pallas import tpu as pltpu
from jax.sharding import PartitionSpec as P

MESH = pl.DeviceIdType.MESH
NLON = 720
KPAD = 1536
B = 128
CH = 144
QT = B // 4
EARLY, LATE = 528, 192
ORDER = [(word[:1], int(word[1:])) for word in (
    "l0", "z1", "z2", "t0", "y0", "w1", "z3", "w2", "z4", "t1", "y1", "t2", "s0", "y2", "h0", "L0", "Z1", "Z2",
    "Z3", "Z4", "w3", "z5", "w4", "z6", "Z5", "Z6", "T0", "Y0", "t3", "s1", "y3", "t4", "s2", "y4", "z7", "Z7",
    "S0", "T1", "Y1", "T2", "Y2", "q0", "p0", "s3", "S1", "q1", "p1", "S2", "q2", "p2", "T3", "Y3", "T4", "Y4",
    "T5", "Y5", "T6", "Y6", "x0", "t5", "y5", "t6", "y6", "s4", "S3", "q3", "p3", "x1", "S4", "q4", "p4", "x2",
    "T7", "Y7", "t7", "y7", "q5", "s5", "S5", "p5", "x3", "q6", "S6", "s6", "p6", "x4", "q7", "S7", "s7", "p7",
    "x5", "x6", "x7",
)]


def row_factors(fields, nlat, nlon):
    lat = (45.0 + 0.5 * (np.arange(nlat) + 0.5 - nlat / 2.0)) * (math.pi / 180.0)
    cosine = np.cos(lat)
    total = fields * nlon * cosine.sum()
    return (np.sqrt(cosine) * total ** (-0.25)).astype(np.float32)


def kernel(x_hbm, lon_ref, lat_ref, fac_ref, o_ref,
           x_ref, coef, halo, v32, sc, rows, a2, part, xin, fin, zin, tot, obuf, minb,
           load_s, halo_s, halo_r, loc_s, z_s, z_r, y_s, y_r, c_s, c_r, x_s, x_r, f_s, f_r,
           o_s, o_r, m_s, m_r):
    snap = lax.axis_index("snap")
    space = lax.axis_index("space")
    z, yl = snap // 2, snap % 2
    xx, yh, core = space // 4, (space // 2) % 2, space % 2
    m_me = space // 2
    same = (core == yl).astype(jnp.int32)
    nb = 4 + same
    kk0 = 1 - same
    off = jnp.where(same == 1, 0, yl)

    def load(j):
        return pltpu.make_async_copy(x_hbm.at[j], x_ref.at[j], load_s.at[j])

    for j in (1, 2, 0, 3, 5, 6, 4, 7):
        load(j).start()

    def copy(src, dst, ss, rs, dev):
        return pltpu.make_async_remote_copy(
            src_ref=src, dst_ref=dst, send_sem=ss, recv_sem=rs, device_id=dev, device_id_type=MESH)

    up_dev = (snap, jnp.maximum(space - 1, 0))
    dn_dev = (snap, jnp.minimum(space + 1, 15))
    y_dev = (z * 2 + 1 - yl, space)
    c_dev = (snap, m_me * 2 + 1 - core)
    h_dev = (snap, xx * 4 + (1 - yh) * 2 + core)

    barrier = pltpu.get_barrier_semaphore()

    def greet(dev):
        pl.semaphore_signal(barrier, inc=1, device_id=dev, device_id_type=MESH)

    for dz in (1, 2, 6, 7):
        greet((((z + dz) % 8) * 2 + yl, space))
    for dx in range(1, 4):
        greet((snap, ((xx + dx) % 4) * 4 + yh * 2 + core))
    greet(y_dev)
    greet(c_dev)
    greet(h_dev)

    @pl.when(space > 0)
    def _():
        greet(up_dev)

    @pl.when(space < 15)
    def _():
        greet(dn_dev)

    def halo_down(f):
        return copy(x_hbm.at[4 * f + 3], halo.at[0, f], halo_s.at[0, f], halo_r.at[0, f], dn_dev)

    def halo_up(f):
        return copy(x_hbm.at[4 * f], halo.at[1, f], halo_s.at[1, f], halo_r.at[1, f], up_dev)

    def span(late):
        return LATE if late else EARLY

    def slot(yy, zz, cc, late):
        return rows.at[yy, zz, pl.ds(pl.multiple_of(cc * NLON + late * EARLY, 16), span(late)), :]

    def stencil(j, place):
        f, row = divmod(j, 4)
        v = x_ref[j].astype(jnp.float32)
        v32[j, pl.ds(8, NLON), :] = v
        v32[j, 7:8, :] = v[NLON - 1:, :]
        v32[j, NLON + 8:NLON + 9, :] = v[:1, :]
        scale = fac_ref[space * 4 + row]
        for s in range(0, NLON, CH):
            a = v32[j, pl.ds(8 + s, CH), :]
            west = v32[j, pl.ds(7 + s, CH), :]
            east = v32[j, pl.ds(9 + s, CH), :]
            if row == 0:
                north = halo[0, f, pl.ds(s, CH), :]
            else:
                north = x_ref[j - 1, pl.ds(s, CH), :]
            if row == 3:
                south = halo[1, f, pl.ds(s, CH), :]
            else:
                south = x_ref[j + 1, pl.ds(s, CH), :]
            lon_part = west + east - 2.0 * a
            lat_part = south.astype(jnp.float32) + north.astype(jnp.float32) - 2.0 * a
            smooth = a + coef[pl.ds(s, CH), j:j + 1] * lon_part + coef[pl.ds(s, CH), 8 + j:9 + j] * lat_part
            sc[pl.ds(place * NLON + s, CH), :] = (smooth * scale).astype(jnp.bfloat16)

    def mine_for(zz, late):
        return sc.at[pl.ds(pl.multiple_of(late * 8 * EARLY + zz * span(late), 16), span(late)), :]

    def z_copy(zz, late):
        return copy(mine_for(zz, late), slot(yl, z, core, late), z_s.at[late, zz], z_r.at[late, z],
                    (zz * 2 + yl, space))

    def local_copy(late):
        return pltpu.make_async_copy(mine_for(z, late), slot(yl, z, core, late), loc_s.at[late])

    def near(i):
        return (z + 8 + ((i + 1) // 2) * (2 * (i % 2) - 1)) % 8

    coef[...] = jnp.concatenate([lon_ref[0], lon_ref[1], lat_ref[0], lat_ref[1]], axis=0).T
    rows[:, :, 2 * NLON:, :] = jnp.zeros((2, 8, KPAD - 2 * NLON, B), jnp.bfloat16)

    @pl.when(space == 0)
    def _():
        halo[0] = jnp.zeros((2, NLON, B), jnp.bfloat16)

    @pl.when(space == 15)
    def _():
        halo[1] = jnp.zeros((2, NLON, B), jnp.bfloat16)

    for j in (1, 2, 0, 3):
        load(j).wait()
    stencil(1, 0)
    stencil(2, 1)
    for j in (5, 6, 4, 7):
        load(j).wait()
    stencil(5, 2)
    stencil(6, 3)

    pl.semaphore_wait(
        barrier,
        10 + (space > 0).astype(jnp.int32) + (space < 15).astype(jnp.int32))

    @pl.when(space < 15)
    def _():
        for f in range(2):
            halo_down(f).start()

    @pl.when(space > 0)
    def _():
        for f in range(2):
            halo_up(f).start()

    @pl.when(core == 0)
    def _():
        for f in range(2):
            halo_up(f).wait_recv()
            stencil(4 * f + 3, 4 + f)

    @pl.when(core == 1)
    def _():
        for f in range(2):
            halo_down(f).wait_recv()
            stencil(4 * f, 4 + f)

    def rest_of_band(n):
        @pl.when(core == 0)
        def _():
            @pl.when(space > 0)
            def _():
                for f in range(2):
                    halo_down(f).wait_recv()

            for f in range(2):
                stencil(4 * f, 6 + f)

        @pl.when(core == 1)
        def _():
            @pl.when(space < 15)
            def _():
                for f in range(2):
                    halo_up(f).wait_recv()

            for f in range(2):
                stencil(4 * f + 3, 6 + f)

    def y_copy(yy, zz, late):
        block = slot(yy, zz, core, late)
        return copy(block, block, y_s.at[late, zz], y_r.at[late, zz], y_dev)

    def c_copy(yy, zz, cc, late):
        block = slot(yy, zz, cc, late)
        return copy(block, block, c_s.at[late, yy, zz], c_r.at[late, yy, zz], c_dev)

    def c_arrive(yy, zz):
        for late in range(2):
            c_copy(yy, zz, 1 - core, late).wait_recv()

    def turn(zz):
        c_arrive(yl, zz)
        a2[blk(zz), :] = rows[yl, zz].T

    def blk(kk):
        return pl.ds(pl.multiple_of(kk * B, B), B)

    def quarter(kk, to):
        return pl.ds(pl.multiple_of(kk * B + to * QT, QT), QT)

    def x_copy(m, kk, dx):
        to = (xx + dx) % 4
        return copy(part.at[m, quarter(kk, to), :], xin.at[m, kk, 3 - dx], x_s.at[m, kk], x_r.at[m, kk],
                    (snap, to * 4 + yh * 2 + core))

    def x_all(m, kk):
        whole = xin.at[m, kk]
        return copy(whole, whole, x_s.at[m, kk], x_r.at[m, kk], (snap, space))

    def z_of(m, kk):
        return (m + 8 - 4 + kk - off) % 8

    def f_start(m, kk, r):
        to, yy = z_of(m, kk), m % 2
        here, there = fin.at[m, kk], zin.at[m // 2, z, yh]

        @pl.when((to == z) & (yy == yh))
        def _():
            pltpu.make_async_copy(here, there, f_r.at[m // 2]).start()

        @pl.when((to != z) | (yy != yh))
        def _():
            copy(here, there, f_s.at[m, kk], f_r.at[m // 2], (to * 2 + yl, xx * 4 + yy * 2 + core)).start()

    def take(n, late):
        zz = near(n)
        if n == 0:
            local_copy(late).wait()
        else:
            block = slot(yl, zz, core, late)
            copy(block, block, z_s.at[late, zz], z_r.at[late, zz], (snap, space)).wait_recv()
        c_copy(yl, zz, core, late).start()

    def share(n, late):
        y_copy(1 - yl, near(n), late).wait_recv()
        c_copy(1 - yl, near(n), core, late).start()

    def pairs(t, use, then, kinds="cr"):
        u = near(t)

        def each(n, what):
            w = near(n)
            k1 = (u + 8 - w - off) % 8
            k2 = (w + 8 - u - off) % 8

            if "c" in kinds:
                @pl.when(k1 < nb)
                def _():
                    what(u, 4 - k1, w)

            if "r" in kinds:
                @pl.when((n < t) & (k2 < nb))
                def _():
                    what(w, 4 - k2, u)

        def one(n, carry):
            each(n, use)

            @pl.when(n > 0)
            def _():
                each(n - 1, then)

            return carry

        lax.fori_loop(0, t + 1, one, 0)
        each(t, then)

    def multiply(m, kk, r):
        part[m, blk(kk), :] = jnp.dot(a2[blk(r), :], rows[core, m], preferred_element_type=jnp.float32)

    def send(m, kk, r):
        for dx in range(1, 4):
            x_copy(m, kk, dx).start()

    def add(m, kk, r):
        x_all(m, kk).wait_recv()
        fin[m, kk] = part[m, quarter(kk, xx), :] + xin[m, kk, 0] + xin[m, kk, 1] + xin[m, kk, 2]

    def row_products(t):
        turn(near(t))
        pairs(t, multiply, send, "r")

    def column_products(t):
        c_arrive(1 - yl, near(t))
        pairs(t, multiply, send, "c")

    def x_sum(t):
        pairs(t, add, f_start)

    actions = {"h": rest_of_band, "q": row_products, "p": column_products, "x": x_sum}
    for late, names in enumerate(("lztysw", "LZTYSW")):
        for name, action in zip(names, (
                lambda n, late: local_copy(late).start(),
                lambda n, late: z_copy(near(n), late).start(),
                take,
                lambda n, late: y_copy(yl, near(n), late).start(),
                share,
                lambda n, late: z_copy(near(n), late).wait_send())):
            actions[name] = functools.partial(action, late=late)
    for name, n in ORDER:
        actions[name](n)

    @pl.when(space < 15)
    def _():
        for f in range(2):
            halo_down(f).wait_send()

    @pl.when(space > 0)
    def _():
        for f in range(2):
            halo_up(f).wait_send()

    for n in range(1, 8):
        for late in range(2):
            if ("wW"[late], n) not in ORDER:
                z_copy(near(n), late).wait_send()

    def drain(zz, carry):
        for late in range(2):
            y_copy(yl, zz, late).wait_send()
            c_copy(0, zz, core, late).wait_send()
            c_copy(1, zz, core, late).wait_send()
        return carry

    lax.fori_loop(0, 8, drain, 0)

    def x_over(kk, carry):
        def one(m, c):
            x_all(m, kk).wait_send()
            return c

        return lax.fori_loop(0, 8, one, carry)

    lax.fori_loop(kk0, 5, x_over, 0)

    def column(n):
        mx = (xx + n) % 4
        m = 2 * mx + yh
        k = (m + 8 - off - z) % 8
        d = 2 * (k + off) + core - yl
        return mx, m, k < nb, (k < nb) & (d >= 1) & (d <= 7)

    rowq = pl.ds(pl.multiple_of(xx * QT, QT), QT)

    def o_copy(n):
        mx, m, _, _ = column(n)
        return copy(tot.at[mx], obuf.at[rowq, :], o_s.at[mx], o_r, (snap, mx * 4 + yh * 2 + core))

    def m_copy(n):
        mx, m, _, _ = column(n)
        return copy(tot.at[mx], minb.at[rowq, :], m_s.at[mx], m_r, (m * 2 + core, snap))

    def whole(n):
        mx, m, mine, mirrored = column(n)

        @pl.when(mine)
        def _():
            pltpu.make_async_copy(zin.at[mx], zin.at[mx], f_r.at[mx]).wait()
            total = zin[mx, 0, 0]
            for zz in range(8):
                for yy in range(2):
                    if zz + yy:
                        total = total + zin[mx, zz, yy]
            tot[mx] = total

    def place(n):
        mx, m, mine, mirrored = column(n)

        @pl.when(mirrored)
        def _():
            m_copy(n).start()

        @pl.when(mine)
        def _():
            if n:
                o_copy(n).start()
            else:
                pltpu.make_async_copy(tot.at[mx], obuf.at[rowq, :], o_r).start()

    whole(2)
    whole(1)
    place(2)
    whole(3)
    place(1)
    whole(0)
    place(3)
    place(0)

    def f_over(kk, carry):
        def one(m, c):
            @pl.when((z_of(m, kk) != z) | (m % 2 != yh))
            def _():
                copy(fin.at[m, kk], fin.at[m, kk], f_s.at[m, kk], f_r.at[0], (snap, space)).wait_send()

            return c

        return lax.fori_loop(0, 8, one, carry)

    lax.fori_loop(kk0, 5, f_over, 0)

    for n in range(4):
        mx, m, mine, mirrored = column(n)

        @pl.when(mirrored)
        def _():
            m_copy(n).wait_send()

        if n:
            @pl.when(mine)
            def _():
                o_copy(n).wait_send()

    k_me = (m_me + 8 - off - z) % 8

    @pl.when(k_me < nb)
    def _():
        pltpu.make_async_copy(obuf, obuf, o_r).wait()
        o_ref[...] = obuf[...]

    @pl.when(k_me >= nb)
    def _():
        pltpu.make_async_copy(minb, minb, m_r).wait()
        o_ref[...] = minb[...].T


def shards(factors, snapshots, lon_coeff, lat_coeff):
    x = jnp.transpose(snapshots, (1, 2, 3, 0)).reshape(8, NLON, B)
    dma = pltpu.SemaphoreType.DMA
    vmem = pl.BlockSpec(memory_space=pltpu.VMEM)
    bf, f32 = jnp.bfloat16, jnp.float32
    return pl.pallas_call(
        kernel,
        out_shape=jax.ShapeDtypeStruct((B, B), f32),
        in_specs=[pl.BlockSpec(memory_space=pl.ANY), vmem, vmem, pl.BlockSpec(memory_space=pltpu.SMEM)],
        out_specs=vmem,
        scratch_shapes=[
            pltpu.VMEM((8, NLON, B), bf),
            pltpu.VMEM((NLON, 16), f32),
            pltpu.VMEM((2, 2, NLON, B), bf),
            pltpu.VMEM((8, NLON + 16, B), f32),
            pltpu.VMEM((8 * NLON, B), bf),
            pltpu.VMEM((2, 8, KPAD, B), bf),
            pltpu.VMEM((8 * B, KPAD), bf),
            pltpu.VMEM((8, 5 * B, B), f32),
            pltpu.VMEM((8, 5, 3, QT, B), f32),
            pltpu.VMEM((8, 5, QT, B), f32),
            pltpu.VMEM((4, 8, 2, QT, B), f32),
            pltpu.VMEM((4, QT, B), f32),
            pltpu.VMEM((B, B), f32),
            pltpu.VMEM((B, B), f32),
            dma((8,)), dma((2, 2)), dma((2, 2)), dma((2,)),
            dma((2, 8)), dma((2, 8)),
            dma((2, 8)), dma((2, 8)),
            dma((2, 2, 8)), dma((2, 2, 8)),
            dma((8, 5)), dma((8, 5)),
            dma((8, 5)), dma((4,)),
            dma((4,)), dma, dma((4,)), dma,
        ],
        compiler_params=pltpu.CompilerParams(collective_id=0, has_side_effects=True),
        name="gram",
    )(x, lon_coeff, lat_coeff, jnp.asarray(factors))


def solution(mesh):
    factors = row_factors(2, 64, NLON)
    return jax.shard_map(
        functools.partial(shards, factors),
        mesh=mesh,
        in_specs=(P("snap", None, "space", None), P(None, "space", None), P(None, "space", None)),
        out_specs=P("snap", "space"),
        check_vma=False,
    )
```

```python
import functools
import math

import jax
import jax.numpy as jnp
import numpy as np
from jax import lax
from jax.experimental import pallas as pl
from jax.experimental.pallas import tpu as pltpu
from jax.sharding import PartitionSpec as P

MESH = pl.DeviceIdType.MESH
NLON = 720
KPAD = 1536
B = 128
CH = 144
QT = B // 4
EARLY, LATE = 528, 192
ORDER = [(word[:1], int(word[1:])) for word in (
    "l0", "z1", "z2", "t0", "y0", "w1", "z3", "w2", "z4", "t1", "y1", "t2", "y2", "s0", "h0", "L0", "Z1", "Z2",
    "Z3", "Z4", "w3", "z5", "w4", "z6", "Z5", "Z6", "T0", "Y0", "T1", "Y1", "T2", "Y2", "t3", "s1", "y3", "t4",
    "s2", "y4", "z7", "Z7", "S0", "p0", "S1", "p1", "S2", "p2", "T3", "Y3", "T4", "Y4", "s3", "T5", "Y5", "T6",
    "Y6", "x0", "t5", "y5", "t6", "y6", "s4", "S3", "p3", "x1", "S4", "p4", "x2", "T7", "Y7", "t7", "y7", "s5",
    "S5", "p5", "x3", "S6", "s6", "p6", "x4", "S7", "s7", "p7", "x5", "x6", "x7",
)]


def row_factors(fields, nlat, nlon):
    lat = (45.0 + 0.5 * (np.arange(nlat) + 0.5 - nlat / 2.0)) * (math.pi / 180.0)
    cosine = np.cos(lat)
    total = fields * nlon * cosine.sum()
    return (np.sqrt(cosine) * total ** (-0.25)).astype(np.float32)


def kernel(x_hbm, lon_ref, lat_ref, fac_ref, o_ref,
           x_ref, coef, halo, v32, sc, rows, a2, part, xin, fin, zin, tot, obuf, minb,
           load_s, halo_s, halo_r, loc_s, z_s, z_r, y_s, y_r, c_s, c_r, x_s, x_r, f_s, f_r,
           o_s, o_r, m_s, m_r):
    snap = lax.axis_index("snap")
    space = lax.axis_index("space")
    z, yl = snap // 2, snap % 2
    xx, yh, core = space // 4, (space // 2) % 2, space % 2
    m_me = space // 2
    same = (core == yl).astype(jnp.int32)
    nb = 4 + same
    kk0 = 1 - same
    off = jnp.where(same == 1, 0, yl)

    def load(j):
        return pltpu.make_async_copy(x_hbm.at[j], x_ref.at[j], load_s.at[j])

    for j in (1, 2, 0, 3, 5, 6, 4, 7):
        load(j).start()

    def copy(src, dst, ss, rs, dev):
        return pltpu.make_async_remote_copy(
            src_ref=src, dst_ref=dst, send_sem=ss, recv_sem=rs, device_id=dev, device_id_type=MESH)

    up_dev = (snap, jnp.maximum(space - 1, 0))
    dn_dev = (snap, jnp.minimum(space + 1, 15))
    y_dev = (z * 2 + 1 - yl, space)
    c_dev = (snap, m_me * 2 + 1 - core)
    h_dev = (snap, xx * 4 + (1 - yh) * 2 + core)

    barrier = pltpu.get_barrier_semaphore()

    def greet(dev):
        pl.semaphore_signal(barrier, inc=1, device_id=dev, device_id_type=MESH)

    for dz in (1, 2, 6, 7):
        greet((((z + dz) % 8) * 2 + yl, space))
    for dx in range(1, 4):
        greet((snap, ((xx + dx) % 4) * 4 + yh * 2 + core))
    greet(y_dev)
    greet(c_dev)
    greet(h_dev)

    @pl.when(space > 0)
    def _():
        greet(up_dev)

    @pl.when(space < 15)
    def _():
        greet(dn_dev)

    def halo_down(f):
        return copy(x_hbm.at[4 * f + 3], halo.at[0, f], halo_s.at[0, f], halo_r.at[0, f], dn_dev)

    def halo_up(f):
        return copy(x_hbm.at[4 * f], halo.at[1, f], halo_s.at[1, f], halo_r.at[1, f], up_dev)

    def span(late):
        return LATE if late else EARLY

    def slot(yy, zz, cc, late):
        return rows.at[yy, zz, pl.ds(pl.multiple_of(cc * NLON + late * EARLY, 16), span(late)), :]

    def stencil(j, place):
        f, row = divmod(j, 4)
        v = x_ref[j].astype(jnp.float32)
        v32[j, pl.ds(8, NLON), :] = v
        v32[j, 7:8, :] = v[NLON - 1:, :]
        v32[j, NLON + 8:NLON + 9, :] = v[:1, :]
        scale = fac_ref[space * 4 + row]
        for s in range(0, NLON, CH):
            a = v32[j, pl.ds(8 + s, CH), :]
            west = v32[j, pl.ds(7 + s, CH), :]
            east = v32[j, pl.ds(9 + s, CH), :]
            if row == 0:
                north = halo[0, f, pl.ds(s, CH), :]
            else:
                north = x_ref[j - 1, pl.ds(s, CH), :]
            if row == 3:
                south = halo[1, f, pl.ds(s, CH), :]
            else:
                south = x_ref[j + 1, pl.ds(s, CH), :]
            lon_part = west + east - 2.0 * a
            lat_part = south.astype(jnp.float32) + north.astype(jnp.float32) - 2.0 * a
            smooth = a + coef[pl.ds(s, CH), j:j + 1] * lon_part + coef[pl.ds(s, CH), 8 + j:9 + j] * lat_part
            sc[pl.ds(place * NLON + s, CH), :] = (smooth * scale).astype(jnp.bfloat16)

    def mine_for(zz, late):
        return sc.at[pl.ds(pl.multiple_of(late * 8 * EARLY + zz * span(late), 16), span(late)), :]

    def z_copy(zz, late):
        return copy(mine_for(zz, late), slot(yl, z, core, late), z_s.at[late, zz], z_r.at[late, z],
                    (zz * 2 + yl, space))

    def local_copy(late):
        return pltpu.make_async_copy(mine_for(z, late), slot(yl, z, core, late), loc_s.at[late])

    def near(i):
        return (z + 8 + ((i + 1) // 2) * (2 * (i % 2) - 1)) % 8

    coef[...] = jnp.concatenate([lon_ref[0], lon_ref[1], lat_ref[0], lat_ref[1]], axis=0).T
    rows[:, :, 2 * NLON:, :] = jnp.zeros((2, 8, KPAD - 2 * NLON, B), jnp.bfloat16)

    @pl.when(space == 0)
    def _():
        halo[0] = jnp.zeros((2, NLON, B), jnp.bfloat16)

    @pl.when(space == 15)
    def _():
        halo[1] = jnp.zeros((2, NLON, B), jnp.bfloat16)

    for j in (1, 2, 0, 3):
        load(j).wait()
    stencil(1, 0)
    stencil(2, 1)
    for j in (5, 6, 4, 7):
        load(j).wait()
    stencil(5, 2)
    stencil(6, 3)

    pl.semaphore_wait(
        barrier,
        10 + (space > 0).astype(jnp.int32) + (space < 15).astype(jnp.int32))

    @pl.when(space < 15)
    def _():
        for f in range(2):
            halo_down(f).start()

    @pl.when(space > 0)
    def _():
        for f in range(2):
            halo_up(f).start()

    @pl.when(core == 0)
    def _():
        for f in range(2):
            halo_up(f).wait_recv()
            stencil(4 * f + 3, 4 + f)

    @pl.when(core == 1)
    def _():
        for f in range(2):
            halo_down(f).wait_recv()
            stencil(4 * f, 4 + f)

    def rest_of_band(n):
        @pl.when(core == 0)
        def _():
            @pl.when(space > 0)
            def _():
                for f in range(2):
                    halo_down(f).wait_recv()

            for f in range(2):
                stencil(4 * f, 6 + f)

        @pl.when(core == 1)
        def _():
            @pl.when(space < 15)
            def _():
                for f in range(2):
                    halo_up(f).wait_recv()

            for f in range(2):
                stencil(4 * f + 3, 6 + f)

    def y_copy(yy, zz, late):
        block = slot(yy, zz, core, late)
        return copy(block, block, y_s.at[late, zz], y_r.at[late, zz], y_dev)

    def c_copy(yy, zz, cc, late):
        block = slot(yy, zz, cc, late)
        return copy(block, block, c_s.at[late, yy, zz], c_r.at[late, yy, zz], c_dev)

    def c_arrive(yy, zz):
        for late in range(2):
            c_copy(yy, zz, 1 - core, late).wait_recv()

    def turn(zz):
        c_arrive(yl, zz)
        a2[blk(zz), :] = rows[yl, zz].T

    def blk(kk):
        return pl.ds(pl.multiple_of(kk * B, B), B)

    def quarter(kk, to):
        return pl.ds(pl.multiple_of(kk * B + to * QT, QT), QT)

    def x_copy(m, kk, dx):
        to = (xx + dx) % 4
        return copy(part.at[m, quarter(kk, to), :], xin.at[m, kk, 3 - dx], x_s.at[m, kk], x_r.at[m, kk],
                    (snap, to * 4 + yh * 2 + core))

    def x_all(m, kk):
        whole = xin.at[m, kk]
        return copy(whole, whole, x_s.at[m, kk], x_r.at[m, kk], (snap, space))

    def z_of(m, kk):
        return (m + 8 - 4 + kk - off) % 8

    def f_start(m, kk, r):
        to, yy = z_of(m, kk), m % 2
        here, there = fin.at[m, kk], zin.at[m // 2, z, yh]

        @pl.when((to == z) & (yy == yh))
        def _():
            pltpu.make_async_copy(here, there, f_r.at[m // 2]).start()

        @pl.when((to != z) | (yy != yh))
        def _():
            copy(here, there, f_s.at[m, kk], f_r.at[m // 2], (to * 2 + yl, xx * 4 + yy * 2 + core)).start()

    def take(n, late):
        zz = near(n)
        if n == 0:
            local_copy(late).wait()
        else:
            block = slot(yl, zz, core, late)
            copy(block, block, z_s.at[late, zz], z_r.at[late, zz], (snap, space)).wait_recv()
        c_copy(yl, zz, core, late).start()

    def share(n, late):
        y_copy(1 - yl, near(n), late).wait_recv()
        c_copy(1 - yl, near(n), core, late).start()

    def pairs(t, use, then):
        u = near(t)

        def each(n, what):
            w = near(n)
            k1 = (u + 8 - w - off) % 8
            k2 = (w + 8 - u - off) % 8

            @pl.when(k1 < nb)
            def _():
                what(u, 4 - k1, w)

            @pl.when((n < t) & (k2 < nb))
            def _():
                what(w, 4 - k2, u)

        def one(n, carry):
            each(n, use)

            @pl.when(n > 0)
            def _():
                each(n - 1, then)

            return carry

        lax.fori_loop(0, t + 1, one, 0)
        each(t, then)

    def multiply(m, kk, r):
        part[m, blk(kk), :] = jnp.dot(a2[blk(r), :], rows[core, m], preferred_element_type=jnp.float32)

    def send(m, kk, r):
        for dx in range(1, 4):
            x_copy(m, kk, dx).start()

    def add(m, kk, r):
        x_all(m, kk).wait_recv()
        fin[m, kk] = part[m, quarter(kk, xx), :] + xin[m, kk, 0] + xin[m, kk, 1] + xin[m, kk, 2]

    def products(t):
        turn(near(t))
        c_arrive(1 - yl, near(t))
        pairs(t, multiply, send)

    def x_sum(t):
        pairs(t, add, f_start)

    actions = {"h": rest_of_band, "p": products, "x": x_sum}
    for late, names in enumerate(("lztysw", "LZTYSW")):
        for name, action in zip(names, (
                lambda n, late: local_copy(late).start(),
                lambda n, late: z_copy(near(n), late).start(),
                take,
                lambda n, late: y_copy(yl, near(n), late).start(),
                share,
                lambda n, late: z_copy(near(n), late).wait_send())):
            actions[name] = functools.partial(action, late=late)
    for name, n in ORDER:
        actions[name](n)

    @pl.when(space < 15)
    def _():
        for f in range(2):
            halo_down(f).wait_send()

    @pl.when(space > 0)
    def _():
        for f in range(2):
            halo_up(f).wait_send()

    for n in range(1, 8):
        for late in range(2):
            if ("wW"[late], n) not in ORDER:
                z_copy(near(n), late).wait_send()

    def drain(zz, carry):
        for late in range(2):
            y_copy(yl, zz, late).wait_send()
            c_copy(0, zz, core, late).wait_send()
            c_copy(1, zz, core, late).wait_send()
        return carry

    lax.fori_loop(0, 8, drain, 0)

    def x_over(kk, carry):
        def one(m, c):
            x_all(m, kk).wait_send()
            return c

        return lax.fori_loop(0, 8, one, carry)

    lax.fori_loop(kk0, 5, x_over, 0)

    def column(n):
        mx = (xx + n) % 4
        m = 2 * mx + yh
        k = (m + 8 - off - z) % 8
        d = 2 * (k + off) + core - yl
        return mx, m, k < nb, (k < nb) & (d >= 1) & (d <= 7)

    rowq = pl.ds(pl.multiple_of(xx * QT, QT), QT)

    def o_copy(n):
        mx, m, _, _ = column(n)
        return copy(tot.at[mx], obuf.at[rowq, :], o_s.at[mx], o_r, (snap, mx * 4 + yh * 2 + core))

    def m_copy(n):
        mx, m, _, _ = column(n)
        return copy(tot.at[mx], minb.at[rowq, :], m_s.at[mx], m_r, (m * 2 + core, snap))

    def whole(n):
        mx, m, mine, mirrored = column(n)

        @pl.when(mine)
        def _():
            pltpu.make_async_copy(zin.at[mx], zin.at[mx], f_r.at[mx]).wait()
            total = zin[mx, 0, 0]
            for zz in range(8):
                for yy in range(2):
                    if zz + yy:
                        total = total + zin[mx, zz, yy]
            tot[mx] = total

    def place(n):
        mx, m, mine, mirrored = column(n)

        @pl.when(mirrored)
        def _():
            m_copy(n).start()

        @pl.when(mine)
        def _():
            if n:
                o_copy(n).start()
            else:
                pltpu.make_async_copy(tot.at[mx], obuf.at[rowq, :], o_r).start()

    whole(2)
    whole(1)
    place(2)
    whole(3)
    place(1)
    whole(0)
    place(3)
    place(0)

    def f_over(kk, carry):
        def one(m, c):
            @pl.when((z_of(m, kk) != z) | (m % 2 != yh))
            def _():
                copy(fin.at[m, kk], fin.at[m, kk], f_s.at[m, kk], f_r.at[0], (snap, space)).wait_send()

            return c

        return lax.fori_loop(0, 8, one, carry)

    lax.fori_loop(kk0, 5, f_over, 0)

    for n in range(4):
        mx, m, mine, mirrored = column(n)

        @pl.when(mirrored)
        def _():
            m_copy(n).wait_send()

        if n:
            @pl.when(mine)
            def _():
                o_copy(n).wait_send()

    k_me = (m_me + 8 - off - z) % 8

    @pl.when(k_me < nb)
    def _():
        pltpu.make_async_copy(obuf, obuf, o_r).wait()
        o_ref[...] = obuf[...]

    @pl.when(k_me >= nb)
    def _():
        pltpu.make_async_copy(minb, minb, m_r).wait()
        o_ref[...] = minb[...].T


def shards(factors, snapshots, lon_coeff, lat_coeff):
    x = jnp.transpose(snapshots, (1, 2, 3, 0)).reshape(8, NLON, B)
    dma = pltpu.SemaphoreType.DMA
    vmem = pl.BlockSpec(memory_space=pltpu.VMEM)
    bf, f32 = jnp.bfloat16, jnp.float32
    return pl.pallas_call(
        kernel,
        out_shape=jax.ShapeDtypeStruct((B, B), f32),
        in_specs=[pl.BlockSpec(memory_space=pl.ANY), vmem, vmem, pl.BlockSpec(memory_space=pltpu.SMEM)],
        out_specs=vmem,
        scratch_shapes=[
            pltpu.VMEM((8, NLON, B), bf),
            pltpu.VMEM((NLON, 16), f32),
            pltpu.VMEM((2, 2, NLON, B), bf),
            pltpu.VMEM((8, NLON + 16, B), f32),
            pltpu.VMEM((8 * NLON, B), bf),
            pltpu.VMEM((2, 8, KPAD, B), bf),
            pltpu.VMEM((8 * B, KPAD), bf),
            pltpu.VMEM((8, 5 * B, B), f32),
            pltpu.VMEM((8, 5, 3, QT, B), f32),
            pltpu.VMEM((8, 5, QT, B), f32),
            pltpu.VMEM((4, 8, 2, QT, B), f32),
            pltpu.VMEM((4, QT, B), f32),
            pltpu.VMEM((B, B), f32),
            pltpu.VMEM((B, B), f32),
            dma((8,)), dma((2, 2)), dma((2, 2)), dma((2,)),
            dma((2, 8)), dma((2, 8)),
            dma((2, 8)), dma((2, 8)),
            dma((2, 2, 8)), dma((2, 2, 8)),
            dma((8, 5)), dma((8, 5)),
            dma((8, 5)), dma((4,)),
            dma((4,)), dma, dma((4,)), dma,
        ],
        compiler_params=pltpu.CompilerParams(collective_id=0, has_side_effects=True),
        name="gram",
    )(x, lon_coeff, lat_coeff, jnp.asarray(factors))


def solution(mesh):
    factors = row_factors(2, 64, NLON)
    return jax.shard_map(
        functools.partial(shards, factors),
        mesh=mesh,
        in_specs=(P("snap", None, "space", None), P(None, "space", None), P(None, "space", None)),
        out_specs=P("snap", "space"),
        check_vma=False,
    )
```

```python
import functools
import math

import jax
import jax.numpy as jnp
import numpy as np
from jax import lax
from jax.experimental import pallas as pl
from jax.experimental.pallas import tpu as pltpu
from jax.sharding import PartitionSpec as P

MESH = pl.DeviceIdType.MESH
NLON = 720
KPAD = 1536
B = 128
CH = 144
QT = B // 4
EARLY, LATE = 528, 192
ORDER = [(word[:1], int(word[1:])) for word in (
    "l0", "z1", "z2", "t0", "y0", "w1", "z3", "w2", "z4", "h0", "L0", "Z1", "Z2", "t1", "y1", "t2", "s0", "y2",
    "Z3", "Z4", "w3", "z5", "w4", "z6", "Z5", "Z6", "T0", "Y0", "t3", "s1", "y3", "t4", "s2", "y4", "z7", "Z7",
    "S0", "T1", "Y1", "T2", "Y2", "p0", "s3", "S1", "p1", "S2", "p2", "T3", "Y3", "T4", "Y4", "T5", "Y5", "T6",
    "Y6", "x0", "t5", "y5", "t6", "y6", "s4", "S3", "p3", "x1", "S4", "p4", "x2", "T7", "Y7", "t7", "y7", "s5",
    "S5", "p5", "x3", "S6", "s6", "p6", "x4", "S7", "s7", "p7", "x5", "x6", "x7",
)]


def row_factors(fields, nlat, nlon):
    lat = (45.0 + 0.5 * (np.arange(nlat) + 0.5 - nlat / 2.0)) * (math.pi / 180.0)
    cosine = np.cos(lat)
    total = fields * nlon * cosine.sum()
    return (np.sqrt(cosine) * total ** (-0.25)).astype(np.float32)


def kernel(x_hbm, lon_ref, lat_ref, fac_ref, o_ref,
           x_ref, coef, halo, v32, sc, rows, a2, part, xin, fin, zin, tot, obuf, minb,
           load_s, halo_s, halo_r, loc_s, z_s, z_r, y_s, y_r, c_s, c_r, x_s, x_r, f_s, f_r,
           o_s, o_r, m_s, m_r):
    snap = lax.axis_index("snap")
    space = lax.axis_index("space")
    z, yl = snap // 2, snap % 2
    xx, yh, core = space // 4, (space // 2) % 2, space % 2
    m_me = space // 2
    same = (core == yl).astype(jnp.int32)
    nb = 4 + same
    kk0 = 1 - same
    off = jnp.where(same == 1, 0, yl)

    def load(j):
        return pltpu.make_async_copy(x_hbm.at[j], x_ref.at[j], load_s.at[j])

    for j in (1, 2, 0, 3, 5, 6, 4, 7):
        load(j).start()

    def copy(src, dst, ss, rs, dev):
        return pltpu.make_async_remote_copy(
            src_ref=src, dst_ref=dst, send_sem=ss, recv_sem=rs, device_id=dev, device_id_type=MESH)

    up_dev = (snap, jnp.maximum(space - 1, 0))
    dn_dev = (snap, jnp.minimum(space + 1, 15))
    y_dev = (z * 2 + 1 - yl, space)
    c_dev = (snap, m_me * 2 + 1 - core)
    h_dev = (snap, xx * 4 + (1 - yh) * 2 + core)

    barrier = pltpu.get_barrier_semaphore()

    def greet(dev):
        pl.semaphore_signal(barrier, inc=1, device_id=dev, device_id_type=MESH)

    for dz in (1, 2, 6, 7):
        greet((((z + dz) % 8) * 2 + yl, space))
    for dx in range(1, 4):
        greet((snap, ((xx + dx) % 4) * 4 + yh * 2 + core))
    greet(y_dev)
    greet(c_dev)
    greet(h_dev)

    @pl.when(space > 0)
    def _():
        greet(up_dev)

    @pl.when(space < 15)
    def _():
        greet(dn_dev)

    def halo_down(f):
        return copy(x_hbm.at[4 * f + 3], halo.at[0, f], halo_s.at[0, f], halo_r.at[0, f], dn_dev)

    def halo_up(f):
        return copy(x_hbm.at[4 * f], halo.at[1, f], halo_s.at[1, f], halo_r.at[1, f], up_dev)

    def span(late):
        return LATE if late else EARLY

    def slot(yy, zz, cc, late):
        return rows.at[yy, zz, pl.ds(pl.multiple_of(cc * NLON + late * EARLY, 16), span(late)), :]

    def stencil(j, place):
        f, row = divmod(j, 4)
        v = x_ref[j].astype(jnp.float32)
        v32[j, pl.ds(8, NLON), :] = v
        v32[j, 7:8, :] = v[NLON - 1:, :]
        v32[j, NLON + 8:NLON + 9, :] = v[:1, :]
        scale = fac_ref[space * 4 + row]
        for s in range(0, NLON, CH):
            a = v32[j, pl.ds(8 + s, CH), :]
            west = v32[j, pl.ds(7 + s, CH), :]
            east = v32[j, pl.ds(9 + s, CH), :]
            if row == 0:
                north = halo[0, f, pl.ds(s, CH), :]
            else:
                north = x_ref[j - 1, pl.ds(s, CH), :]
            if row == 3:
                south = halo[1, f, pl.ds(s, CH), :]
            else:
                south = x_ref[j + 1, pl.ds(s, CH), :]
            lon_part = west + east - 2.0 * a
            lat_part = south.astype(jnp.float32) + north.astype(jnp.float32) - 2.0 * a
            smooth = a + coef[pl.ds(s, CH), j:j + 1] * lon_part + coef[pl.ds(s, CH), 8 + j:9 + j] * lat_part
            sc[pl.ds(place * NLON + s, CH), :] = (smooth * scale).astype(jnp.bfloat16)

    def mine_for(zz, late):
        return sc.at[pl.ds(pl.multiple_of(late * 8 * EARLY + zz * span(late), 16), span(late)), :]

    def z_copy(zz, late):
        return copy(mine_for(zz, late), slot(yl, z, core, late), z_s.at[late, zz], z_r.at[late, z],
                    (zz * 2 + yl, space))

    def local_copy(late):
        return pltpu.make_async_copy(mine_for(z, late), slot(yl, z, core, late), loc_s.at[late])

    def near(i):
        return (z + 8 + ((i + 1) // 2) * (2 * (i % 2) - 1)) % 8

    coef[...] = jnp.concatenate([lon_ref[0], lon_ref[1], lat_ref[0], lat_ref[1]], axis=0).T
    rows[:, :, 2 * NLON:, :] = jnp.zeros((2, 8, KPAD - 2 * NLON, B), jnp.bfloat16)

    @pl.when(space == 0)
    def _():
        halo[0] = jnp.zeros((2, NLON, B), jnp.bfloat16)

    @pl.when(space == 15)
    def _():
        halo[1] = jnp.zeros((2, NLON, B), jnp.bfloat16)

    for j in (1, 2, 0, 3):
        load(j).wait()
    stencil(1, 0)
    stencil(2, 1)
    for j in (5, 6, 4, 7):
        load(j).wait()
    stencil(5, 2)
    stencil(6, 3)

    pl.semaphore_wait(
        barrier,
        10 + (space > 0).astype(jnp.int32) + (space < 15).astype(jnp.int32))

    @pl.when(space < 15)
    def _():
        for f in range(2):
            halo_down(f).start()

    @pl.when(space > 0)
    def _():
        for f in range(2):
            halo_up(f).start()

    @pl.when(core == 0)
    def _():
        for f in range(2):
            halo_up(f).wait_recv()
            stencil(4 * f + 3, 4 + f)

    @pl.when(core == 1)
    def _():
        for f in range(2):
            halo_down(f).wait_recv()
            stencil(4 * f, 4 + f)

    def rest_of_band(n):
        @pl.when(core == 0)
        def _():
            @pl.when(space > 0)
            def _():
                for f in range(2):
                    halo_down(f).wait_recv()

            for f in range(2):
                stencil(4 * f, 6 + f)

        @pl.when(core == 1)
        def _():
            @pl.when(space < 15)
            def _():
                for f in range(2):
                    halo_up(f).wait_recv()

            for f in range(2):
                stencil(4 * f + 3, 6 + f)

    def y_copy(yy, zz, late):
        block = slot(yy, zz, core, late)
        return copy(block, block, y_s.at[late, zz], y_r.at[late, zz], y_dev)

    def c_copy(yy, zz, cc, late):
        block = slot(yy, zz, cc, late)
        return copy(block, block, c_s.at[late, yy, zz], c_r.at[late, yy, zz], c_dev)

    def c_arrive(yy, zz):
        for late in range(2):
            c_copy(yy, zz, 1 - core, late).wait_recv()

    def turn(zz):
        c_arrive(yl, zz)
        a2[blk(zz), :] = rows[yl, zz].T

    def blk(kk):
        return pl.ds(pl.multiple_of(kk * B, B), B)

    def quarter(kk, to):
        return pl.ds(pl.multiple_of(kk * B + to * QT, QT), QT)

    def x_copy(m, kk, dx):
        to = (xx + dx) % 4
        return copy(part.at[m, quarter(kk, to), :], xin.at[m, kk, 3 - dx], x_s.at[m, kk], x_r.at[m, kk],
                    (snap, to * 4 + yh * 2 + core))

    def x_all(m, kk):
        whole = xin.at[m, kk]
        return copy(whole, whole, x_s.at[m, kk], x_r.at[m, kk], (snap, space))

    def z_of(m, kk):
        return (m + 8 - 4 + kk - off) % 8

    def f_start(m, kk, r):
        to, yy = z_of(m, kk), m % 2
        here, there = fin.at[m, kk], zin.at[m // 2, z, yh]

        @pl.when((to == z) & (yy == yh))
        def _():
            pltpu.make_async_copy(here, there, f_r.at[m // 2]).start()

        @pl.when((to != z) | (yy != yh))
        def _():
            copy(here, there, f_s.at[m, kk], f_r.at[m // 2], (to * 2 + yl, xx * 4 + yy * 2 + core)).start()

    def take(n, late):
        zz = near(n)
        if n == 0:
            local_copy(late).wait()
        else:
            block = slot(yl, zz, core, late)
            copy(block, block, z_s.at[late, zz], z_r.at[late, zz], (snap, space)).wait_recv()
        c_copy(yl, zz, core, late).start()

    def share(n, late):
        y_copy(1 - yl, near(n), late).wait_recv()
        c_copy(1 - yl, near(n), core, late).start()

    def pairs(t, use, then):
        u = near(t)

        def each(n, what):
            w = near(n)
            k1 = (u + 8 - w - off) % 8
            k2 = (w + 8 - u - off) % 8

            @pl.when(k1 < nb)
            def _():
                what(u, 4 - k1, w)

            @pl.when((n < t) & (k2 < nb))
            def _():
                what(w, 4 - k2, u)

        def one(n, carry):
            each(n, use)

            @pl.when(n > 0)
            def _():
                each(n - 1, then)

            return carry

        lax.fori_loop(0, t + 1, one, 0)
        each(t, then)

    def multiply(m, kk, r):
        part[m, blk(kk), :] = jnp.dot(a2[blk(r), :], rows[core, m], preferred_element_type=jnp.float32)

    def send(m, kk, r):
        for dx in range(1, 4):
            x_copy(m, kk, dx).start()

    def add(m, kk, r):
        x_all(m, kk).wait_recv()
        fin[m, kk] = part[m, quarter(kk, xx), :] + xin[m, kk, 0] + xin[m, kk, 1] + xin[m, kk, 2]

    def products(t):
        turn(near(t))
        c_arrive(1 - yl, near(t))
        pairs(t, multiply, send)

    def x_sum(t):
        pairs(t, add, f_start)

    actions = {"h": rest_of_band, "p": products, "x": x_sum}
    for late, names in enumerate(("lztysw", "LZTYSW")):
        for name, action in zip(names, (
                lambda n, late: local_copy(late).start(),
                lambda n, late: z_copy(near(n), late).start(),
                take,
                lambda n, late: y_copy(yl, near(n), late).start(),
                share,
                lambda n, late: z_copy(near(n), late).wait_send())):
            actions[name] = functools.partial(action, late=late)
    for name, n in ORDER:
        actions[name](n)

    @pl.when(space < 15)
    def _():
        for f in range(2):
            halo_down(f).wait_send()

    @pl.when(space > 0)
    def _():
        for f in range(2):
            halo_up(f).wait_send()

    for n in range(1, 8):
        for late in range(2):
            if ("wW"[late], n) not in ORDER:
                z_copy(near(n), late).wait_send()

    def drain(zz, carry):
        for late in range(2):
            y_copy(yl, zz, late).wait_send()
            c_copy(0, zz, core, late).wait_send()
            c_copy(1, zz, core, late).wait_send()
        return carry

    lax.fori_loop(0, 8, drain, 0)

    def x_over(kk, carry):
        def one(m, c):
            x_all(m, kk).wait_send()
            return c

        return lax.fori_loop(0, 8, one, carry)

    lax.fori_loop(kk0, 5, x_over, 0)

    def column(n):
        mx = (xx + n) % 4
        m = 2 * mx + yh
        k = (m + 8 - off - z) % 8
        d = 2 * (k + off) + core - yl
        return mx, m, k < nb, (k < nb) & (d >= 1) & (d <= 7)

    rowq = pl.ds(pl.multiple_of(xx * QT, QT), QT)

    def o_copy(n):
        mx, m, _, _ = column(n)
        return copy(tot.at[mx], obuf.at[rowq, :], o_s.at[mx], o_r, (snap, mx * 4 + yh * 2 + core))

    def m_copy(n):
        mx, m, _, _ = column(n)
        return copy(tot.at[mx], minb.at[rowq, :], m_s.at[mx], m_r, (m * 2 + core, snap))

    def whole(n):
        mx, m, mine, mirrored = column(n)

        @pl.when(mine)
        def _():
            pltpu.make_async_copy(zin.at[mx], zin.at[mx], f_r.at[mx]).wait()
            total = zin[mx, 0, 0]
            for zz in range(8):
                for yy in range(2):
                    if zz + yy:
                        total = total + zin[mx, zz, yy]
            tot[mx] = total

    def place(n):
        mx, m, mine, mirrored = column(n)

        @pl.when(mirrored)
        def _():
            m_copy(n).start()

        @pl.when(mine)
        def _():
            if n:
                o_copy(n).start()
            else:
                pltpu.make_async_copy(tot.at[mx], obuf.at[rowq, :], o_r).start()

    whole(2)
    whole(1)
    place(2)
    whole(3)
    place(1)
    whole(0)
    place(3)
    place(0)

    def f_over(kk, carry):
        def one(m, c):
            @pl.when((z_of(m, kk) != z) | (m % 2 != yh))
            def _():
                copy(fin.at[m, kk], fin.at[m, kk], f_s.at[m, kk], f_r.at[0], (snap, space)).wait_send()

            return c

        return lax.fori_loop(0, 8, one, carry)

    lax.fori_loop(kk0, 5, f_over, 0)

    for n in range(4):
        mx, m, mine, mirrored = column(n)

        @pl.when(mirrored)
        def _():
            m_copy(n).wait_send()

        if n:
            @pl.when(mine)
            def _():
                o_copy(n).wait_send()

    k_me = (m_me + 8 - off - z) % 8

    @pl.when(k_me < nb)
    def _():
        pltpu.make_async_copy(obuf, obuf, o_r).wait()
        o_ref[...] = obuf[...]

    @pl.when(k_me >= nb)
    def _():
        pltpu.make_async_copy(minb, minb, m_r).wait()
        o_ref[...] = minb[...].T


def shards(factors, snapshots, lon_coeff, lat_coeff):
    x = jnp.transpose(snapshots, (1, 2, 3, 0)).reshape(8, NLON, B)
    dma = pltpu.SemaphoreType.DMA
    vmem = pl.BlockSpec(memory_space=pltpu.VMEM)
    bf, f32 = jnp.bfloat16, jnp.float32
    return pl.pallas_call(
        kernel,
        out_shape=jax.ShapeDtypeStruct((B, B), f32),
        in_specs=[pl.BlockSpec(memory_space=pl.ANY), vmem, vmem, pl.BlockSpec(memory_space=pltpu.SMEM)],
        out_specs=vmem,
        scratch_shapes=[
            pltpu.VMEM((8, NLON, B), bf),
            pltpu.VMEM((NLON, 16), f32),
            pltpu.VMEM((2, 2, NLON, B), bf),
            pltpu.VMEM((8, NLON + 16, B), f32),
            pltpu.VMEM((8 * NLON, B), bf),
            pltpu.VMEM((2, 8, KPAD, B), bf),
            pltpu.VMEM((8 * B, KPAD), bf),
            pltpu.VMEM((8, 5 * B, B), f32),
            pltpu.VMEM((8, 5, 3, QT, B), f32),
            pltpu.VMEM((8, 5, QT, B), f32),
            pltpu.VMEM((4, 8, 2, QT, B), f32),
            pltpu.VMEM((4, QT, B), f32),
            pltpu.VMEM((B, B), f32),
            pltpu.VMEM((B, B), f32),
            dma((8,)), dma((2, 2)), dma((2, 2)), dma((2,)),
            dma((2, 8)), dma((2, 8)),
            dma((2, 8)), dma((2, 8)),
            dma((2, 2, 8)), dma((2, 2, 8)),
            dma((8, 5)), dma((8, 5)),
            dma((8, 5)), dma((4,)),
            dma((4,)), dma, dma((4,)), dma,
        ],
        compiler_params=pltpu.CompilerParams(collective_id=0, has_side_effects=True),
        name="gram",
    )(x, lon_coeff, lat_coeff, jnp.asarray(factors))


def solution(mesh):
    factors = row_factors(2, 64, NLON)
    return jax.shard_map(
        functools.partial(shards, factors),
        mesh=mesh,
        in_specs=(P("snap", None, "space", None), P(None, "space", None), P(None, "space", None)),
        out_specs=P("snap", "space"),
        check_vma=False,
    )
```
